256 devices in a mesh: row: 32 (over z, x), col: 8 (over y, core).
Axes of the slice: x: 4, y: 4, z: 8, core: 2. Of those that a mesh axis runs over, the one named last changes fastest.
Arguments:
- panel_transposed: float32 [256, 65536], P('col', 'row'), may hold values from -0.0234375 to 0.0234375
- trailing: float32 [65536, 4096], P('row', 'col'), may hold values from -6 to 6
Outputs:
- stop_factors: float32 [8192, 256], P('row')
- stop_blocks: float32 [8192, 4096], P('row', 'col')
- projected: float32 [65536, 4096], P('row', 'col')
The draws below stay inside these ranges and needn't reach their ends.
All inputs are finite; a program needn't handle non-finite values.
Results may differ from the reference program's by a relative error of at most 0.00026.
Values sent between devices are 32-bit elements; how exact they have to be, the bound alone decides.
No kernel may reach another device: no remote copies, remote signals or barrier semaphores. Data moves between devices by JAX's collectives and lax.ppermute only.
A program may use at most 128 MiB of HBM per device.

```python
import jax
import jax.numpy as jnp
from jax import lax

NB = 256
ROWS_DEV = 2048
ROWS = 65536
NCOLS = 4096
N_ROW = 32


def levels(stream_key, extent, pieces, least, high):
    gain = 1.0
    for axis_at, shards_of in pieces:
        draws = jax.random.uniform(jax.random.fold_in(jax.random.fold_in(stream_key, 6), axis_at), (shards_of,), jnp.float32, least / len(pieces), high / len(pieces))
        gain = gain * jnp.repeat(jnp.exp(draws), extent[axis_at] // shards_of).reshape((-1,) + (1,) * (len(extent) - 1 - axis_at))
    return gain


def normal_values(own_key, extent, deviation, limit, shards=(), held_as=jnp.bfloat16):
    drawn = jax.random.normal(own_key, extent, jnp.float32) * deviation
    if len(shards) > 0:
        drawn = levels(own_key, extent, shards, -0.22, 0.18) * drawn
    return jnp.clip(drawn, min=-limit, max=limit).astype(held_as)


def setup_inputs(seed: int = 0) -> dict:
    keys = jax.random.split(jax.random.key(seed), 3)
    panel_transposed = normal_values(keys[0], (NB, ROWS), ROWS ** -0.5, 0.0234375, ((0, 8), (1, 32)), jnp.float32)
    trailing = normal_values(keys[1], (ROWS, NCOLS), 1.0, 6.0, ((0, 32), (1, 8)), jnp.float32)
    return {"panel_transposed": panel_transposed, "trailing": trailing}


def reference(panel_transposed, trailing):
    highest = lax.Precision.HIGHEST
    panel_blocks = panel_transposed.reshape(NB, N_ROW, ROWS_DEV)
    trail_blocks = trailing.reshape(N_ROW, ROWS_DEV, NCOLS)
    grams = jnp.einsum('asr,bsr->sab', panel_blocks, panel_blocks, precision=highest)
    crosses = jnp.einsum('asr,src->sac', panel_blocks, trail_blocks, precision=highest)
    prefix_gram = jnp.cumsum(grams, axis=0)
    prefix_cross = jnp.cumsum(crosses, axis=0)
    lowers = jnp.linalg.cholesky(prefix_gram)
    stop_blocks = jax.scipy.linalg.solve_triangular(lowers, prefix_cross, lower=True)
    stop_factors = jnp.swapaxes(lowers, 1, 2).reshape(N_ROW * NB, NB)
    coeffs = jax.scipy.linalg.solve_triangular(lowers[-1].T, stop_blocks[-1], lower=False)
    projected = trailing - jnp.einsum('ar,ac->rc', panel_transposed, coeffs, precision=highest)
    return (stop_factors, stop_blocks.reshape(N_ROW * NB, NCOLS), projected)
```

```python
import jax
import jax.numpy as jnp
from jax import lax
from jax.experimental import pallas as pl
from jax.experimental.pallas import tpu as pltpu
from jax.sharding import PartitionSpec as P


HIGHEST = lax.Precision.HIGHEST
F32 = jnp.float32
BF16 = jnp.bfloat16
X = 4


def dot(left, right, dims=(1, 0), precision=HIGHEST):
    return lax.dot_general(
        left,
        right,
        (((dims[0],), (dims[1],)), ((), ())),
        precision=precision,
        preferred_element_type=F32,
    )


def halves(value):
    high = value.astype(BF16)
    return high, (value - high.astype(F32)).astype(BF16)


def dot3(left, right, dims=(1, 0)):
    (lh, ll), (rh, rl) = left, right
    default = lax.Precision.DEFAULT
    return dot(lh, rh, dims, default) + (dot(ll, rh, dims, default) + dot(lh, rl, dims, default))


def room(mebibytes):
    return pltpu.CompilerParams(vmem_limit_bytes=mebibytes * 2**20)


def cost(us):
    return pl.CostEstimate(flops=int(us * 5e8), bytes_accessed=int(us * 1e6), transcendentals=0)


def rotate(value, axis, pairs):
    return lax.ppermute(value, axis, pairs)


def from_chips(value):
    count = lax.axis_size("col")
    sames = [value] + [
        rotate(value, "col", [(i, (i + 2 * k) % count) for i in range(count)]) for k in (1, 3, 2)
    ]
    others = [rotate(v, "col", [(i, i ^ 1) for i in range(count)]) for v in sames]
    return sames + others


def chip_offsets():
    me = lax.axis_index("col")
    count = lax.axis_size("col")
    chip, core = me // 2, lax.rem(me, 2)
    chips = count // 2
    steps = (0, 1, 3, 2)
    return [2 * lax.rem(chip + chips - k, chips) + (core if same else 1 - core) for same in (True, False) for k in steps]


def from_stops_x(value):
    count = lax.axis_size("row")
    return [
        rotate(value, "row", [(i, i - i % X + (i + k) % X) for i in range(count)]) for k in (1, 3, 2)
    ]


def gather_kernel(*refs):
    pieces, (high_ref, low_ref, gram_ref, whole_ref) = refs[:-4], refs[-4:]
    height = pieces[0].shape[0]
    for piece, owner in zip(pieces, chip_offsets()):
        rows = pl.ds(pl.multiple_of(owner * height, height), height)
        value = piece[...]
        whole_ref[rows, :] = value
        high, low = halves(value)
        high_ref[rows, :] = high
        low_ref[rows, :] = low
    gram_ref[...] = dot(pieces[0][...], whole_ref[...], (1, 1))


def gather(pieces):
    height, rows = pieces[0].shape
    width = height * len(pieces)
    shapes = [(width, rows, BF16), (width, rows, BF16), (height, width, F32)]
    return pl.pallas_call(
        gather_kernel,
        out_shape=[jax.ShapeDtypeStruct((a, b), t) for a, b, t in shapes],
        scratch_shapes=[pltpu.VMEM((width, rows), F32)],
        cost_estimate=cost(4),
        compiler_params=room(16),
        name="gather",
    )(*pieces)


def turn_kernel(high_ref, low_ref, high_out, low_out):
    high_out[...] = high_ref[...].T
    low_out[...] = low_ref[...].T


def turn(high, low):
    width, rows = high.shape
    block = 512
    shape = jax.ShapeDtypeStruct((rows, width), BF16)
    return pl.pallas_call(
        turn_kernel,
        grid=(rows // block,),
        in_specs=[pl.BlockSpec((width, block), lambda i: (0, i))] * 2,
        out_specs=[pl.BlockSpec((block, width), lambda i: (i, 0))] * 2,
        out_shape=[shape, shape],
        cost_estimate=cost(3),
        compiler_params=room(8),
        name="turn",
    )(high, low)


def cross_kernel(high_ref, low_ref, trailing_ref, out_ref):
    @pl.when(pl.program_id(0) == 0)
    def _():
        out_ref[...] = jnp.zeros_like(out_ref)

    out_ref[...] += dot3((high_ref[...], low_ref[...]), halves(trailing_ref[...]))


def cross(high, low, trailing):
    width, rows = high.shape
    columns = trailing.shape[1]
    block = 512
    return pl.pallas_call(
        cross_kernel,
        grid=(rows // block,),
        in_specs=[
            pl.BlockSpec((width, block), lambda i: (0, i)),
            pl.BlockSpec((width, block), lambda i: (0, i)),
            pl.BlockSpec((block, columns), lambda i: (i, 0)),
        ],
        out_specs=pl.BlockSpec((width, columns), lambda i: (0, 0)),
        out_shape=jax.ShapeDtypeStruct((width, columns), F32),
        cost_estimate=cost(5),
        compiler_params=room(16),
        name="cross",
    )(high, low, trailing)


def group_kernel(own_ref, one_ref, three_ref, two_ref, prefix_ref, total_ref):
    place = lax.rem(lax.axis_index("row"), X)
    own, one, two, three = own_ref[...], one_ref[...], two_ref[...], three_ref[...]
    prefix_ref[...] = (
        own + jnp.where(place >= 1, one, 0.0) + jnp.where(place >= 2, two, 0.0) + jnp.where(place >= 3, three, 0.0)
    )
    total = (own + one) + (two + three)
    for z in range(total_ref.shape[0]):
        total_ref[z] = total


def group(own, behind, groups):
    return pl.pallas_call(
        group_kernel,
        out_shape=[
            jax.ShapeDtypeStruct(own.shape, F32),
            jax.ShapeDtypeStruct((groups,) + own.shape, F32),
        ],
        cost_estimate=cost(1),
        compiler_params=room(2),
        name="group",
    )(own, *behind)


def groups_kernel(prefix_ref, totals_ref, out_ref):
    place = lax.div(lax.axis_index("row"), X)
    before = prefix_ref[...]
    total = totals_ref[0]
    for z in range(totals_ref.shape[0]):
        before = before + jnp.where(place > z, totals_ref[z], 0.0)
        if z:
            total = total + totals_ref[z]
    out_ref[0] = before
    out_ref[1] = total


def groups(prefix, totals):
    return pl.pallas_call(
        groups_kernel,
        out_shape=jax.ShapeDtypeStruct((2,) + prefix.shape, F32),
        cost_estimate=cost(1),
        compiler_params=room(2),
        name="groups",
    )(prefix, totals)


def scan_kernel(pieces_ref, out_ref):
    stops, height, _ = pieces_ref.shape
    total = pieces_ref[0]
    out_ref[0, :height] = total
    for s in range(1, stops):
        total = total + pieces_ref[s]
        out_ref[s, :height] = total
    for s in range(stops):
        out_ref[s, height:] = total


def scan(pieces):
    stops, height, columns = pieces.shape
    return pl.pallas_call(
        scan_kernel,
        out_shape=jax.ShapeDtypeStruct((stops, 2 * height, columns), F32),
        cost_estimate=cost(1),
        compiler_params=room(4),
        name="scan",
    )(pieces)


def eliminate(matrices):
    order = matrices[0].shape[0]
    count = order // 8
    full = (8, order)
    lane = lax.broadcasted_iota(jnp.int32, full, 1)
    sublane = lax.broadcasted_iota(jnp.int32, full, 0)
    grids = [[m[8 * g : 8 * g + 8, :] for g in range(count)] for m in matrices]
    for p in range(count):
        start = 8 * p
        inside = (lane >= start) & (lane < start + 8)
        for grid in grids:
            block = grid[p]
            columns = [jnp.broadcast_to(block[:, start + c : start + c + 1], full) for c in range(8)]
            entry = [[None] * r + [jnp.broadcast_to(columns[r][c : c + 1, :], full) for c in range(r, 8)] for r in range(8)]
            rows = [jnp.broadcast_to(block[r : r + 1, :], full) for r in range(8)]
            rows = [jnp.where(inside, jnp.where(lane == start + r, 1.0, 0.0), rows[r]) for r in range(8)]
            inverse, multiple = [], [[None] * 8 for _ in range(8)]
            for k in range(8):
                inverse.append(1.0 / entry[k][k])
                for r in range(k + 1, 8):
                    multiple[r][k] = entry[k][r] * inverse[k]
                for r in range(k + 1, 8):
                    for c in range(r, 8):
                        entry[r][c] = entry[r][c] - multiple[r][k] * entry[k][c]
                    rows[r] = rows[r] - multiple[r][k] * rows[k]
            result = rows[0]
            for r in range(1, 8):
                result = jnp.where(sublane == r, rows[r], result)
            for c in range(8):
                column = entry[0][c]
                for r in range(1, c + 1):
                    column = jnp.where(sublane == r, entry[r][c], column)
                result = jnp.where((lane == start + c) & (sublane <= c), column, result)
            if p < count - 1:
                solved = [rows[k] * inverse[k] for k in range(8)]
                for k in range(6, -1, -1):
                    for r in range(k + 1, 8):
                        solved[k] = solved[k] - multiple[r][k] * solved[r]
                for g in range(p + 1, count):
                    value = jnp.where(inside, 0.0, grid[g])
                    for k in range(8):
                        value = value - jnp.broadcast_to(grid[g][:, start + k : start + k + 1], full) * solved[k]
                    grid[g] = value
            grid[p] = result
    return [jnp.concatenate(grid, 0) for grid in grids]


def split(reduced):
    order = reduced.shape[0]
    row = lax.broadcasted_iota(jnp.int32, (order, order), 0)
    column = lax.broadcasted_iota(jnp.int32, (order, order), 1)
    pivots = jnp.sum(jnp.where(row == column, reduced, 0.0), axis=1, keepdims=True)
    scale = lax.rsqrt(pivots)
    upper = jnp.where(row <= column, reduced, 0.0) * scale
    lower = jnp.where(row > column, reduced, jnp.where(row == column, 1.0, 0.0)) * scale
    return upper, lower


def factor_kernel(*refs):
    pieces, (upper_ref, inverse_ref, gram_ref) = refs[:-3], refs[-3:]
    count, height, order = pieces[0].shape
    half = order // 2
    for piece, owner in zip(pieces, chip_offsets()):
        gram_ref[:, pl.ds(pl.multiple_of(owner * height, height), height), :] = piece[...]
    tops = eliminate([gram_ref[i, :half, :half] for i in range(count)])
    schurs, sides = [], []
    for i, reduced in enumerate(tops):
        upper, inverse = split(reduced)
        across = dot(inverse, gram_ref[i, :half, half:])
        side = dot(gram_ref[i, half:, :half], inverse, (1, 1))
        schurs.append(gram_ref[i, half:, half:] - dot(side, across))
        sides.append(dot(side, inverse))
        if i == 0:
            upper_ref[:half, :half] = upper
            upper_ref[:half, half:] = across
            upper_ref[half:, :half] = jnp.zeros((half, half), F32)
        inverse_ref[i, :half, :half] = inverse
        inverse_ref[i, :half, half:] = jnp.zeros((half, half), F32)
    for i, reduced in enumerate(eliminate(schurs)):
        upper, inverse = split(reduced)
        if i == 0:
            upper_ref[half:, half:] = upper
        inverse_ref[i, half:, half:] = inverse
        inverse_ref[i, half:, :half] = -dot(inverse, sides[i])


def factor(pieces):
    count, height, order = pieces[0].shape
    return pl.pallas_call(
        factor_kernel,
        out_shape=[
            jax.ShapeDtypeStruct((order, order), F32),
            jax.ShapeDtypeStruct((count, order, order), F32),
        ],
        scratch_shapes=[pltpu.VMEM((count, order, order), F32)],
        cost_estimate=cost(16),
        compiler_params=room(8),
        name="factor",
    )(*pieces)


def project_kernel(inverse_ref, sums_ref, high_ref, low_ref, trailing_ref, blocks_ref, out_ref, ch_ref, cl_ref):
    @pl.when(pl.program_id(0) == 0)
    def _():
        stops, both, columns = sums_ref.shape
        height = both // 2
        own = halves(inverse_ref[0])
        last = halves(inverse_ref[1])
        total = sums_ref[:, height:, :].reshape(stops * height, columns)
        last_block = dot3(last, halves(total))
        high, low = halves(dot3(last, halves(last_block), (0, 0)))
        ch_ref[...] = high
        cl_ref[...] = low
        prefix = sums_ref[:, :height, :].reshape(stops * height, columns)
        blocks_ref[...] = dot3(own, halves(prefix))

    out_ref[...] = trailing_ref[...] - dot3((high_ref[...], low_ref[...]), (ch_ref[...], cl_ref[...]))


def project(inverses, sums, high, low, trailing):
    rows, columns = trailing.shape
    width = high.shape[1]
    block = 256
    return pl.pallas_call(
        project_kernel,
        grid=(rows // block,),
        in_specs=[
            pl.BlockSpec(inverses.shape, lambda i: (0, 0, 0)),
            pl.BlockSpec(sums.shape, lambda i: (0, 0, 0)),
            pl.BlockSpec((block, width), lambda i: (i, 0)),
            pl.BlockSpec((block, width), lambda i: (i, 0)),
            pl.BlockSpec((block, columns), lambda i: (i, 0)),
        ],
        out_specs=[
            pl.BlockSpec((width, columns), lambda i: (0, 0)),
            pl.BlockSpec((block, columns), lambda i: (i, 0)),
        ],
        out_shape=[
            jax.ShapeDtypeStruct((width, columns), F32),
            jax.ShapeDtypeStruct((rows, columns), F32),
        ],
        scratch_shapes=[pltpu.VMEM((width, columns), BF16)] * 2,
        cost_estimate=cost(8),
        compiler_params=room(16),
        name="project",
    )(inverses, sums, high, low, trailing)


def shards(panel_transposed, trailing):
    stops = lax.axis_size("row")
    high, low, own_gram = gather(from_chips(panel_transposed))
    width = high.shape[0]
    columns = trailing.shape[1]

    behind = from_stops_x(own_gram)
    own_cross = cross(high, low, trailing)
    pieces = lax.all_to_all(own_cross.reshape(stops, width // stops, columns), "row", 0, 0, tiled=True)

    prefix, totals = group(own_gram, behind, stops // X)
    same_x = [[z * X + x for z in range(stops // X)] for x in range(X)]
    totals = lax.all_to_all(totals, "row", 0, 0, tiled=True, axis_index_groups=same_x)
    grams = from_chips(groups(prefix, totals))
    high, low = turn(high, low)

    both = scan(pieces)
    sums = lax.all_to_all(both, "row", 0, 0, tiled=True)
    grams, both = lax.optimization_barrier((grams, both))
    stop_factors, inverses = factor(grams)
    stop_blocks, projected = project(inverses, sums, high, low, trailing)
    return (stop_factors, stop_blocks, projected)


def solution(mesh):
    return jax.shard_map(
        shards,
        mesh=mesh,
        in_specs=(P("col", "row"), P("row", "col")),
        out_specs=(P("row", None), P("row", "col"), P("row", "col")),
        check_vma=False,
    )
```

```python
import jax
import jax.numpy as jnp
from jax import lax
from jax.experimental import pallas as pl
from jax.experimental.pallas import tpu as pltpu
from jax.sharding import PartitionSpec as P


HIGHEST = lax.Precision.HIGHEST
F32 = jnp.float32
BF16 = jnp.bfloat16
X = 4


def dot(left, right, dims=(1, 0), precision=HIGHEST):
    return lax.dot_general(
        left,
        right,
        (((dims[0],), (dims[1],)), ((), ())),
        precision=precision,
        preferred_element_type=F32,
    )


def halves(value):
    high = value.astype(BF16)
    return high, (value - high.astype(F32)).astype(BF16)


def dot3(left, right, dims=(1, 0)):
    (lh, ll), (rh, rl) = left, right
    default = lax.Precision.DEFAULT
    return dot(lh, rh, dims, default) + (dot(ll, rh, dims, default) + dot(lh, rl, dims, default))


def room(mebibytes):
    return pltpu.CompilerParams(vmem_limit_bytes=mebibytes * 2**20)


def cost(us):
    return pl.CostEstimate(flops=int(us * 5e8), bytes_accessed=int(us * 1e6), transcendentals=0)


def rotate(value, axis, pairs):
    return lax.ppermute(value, axis, pairs)


def from_chips(value):
    count = lax.axis_size("col")
    sames = [value] + [
        rotate(value, "col", [(i, (i + 2 * k) % count) for i in range(count)]) for k in (1, 3, 2)
    ]
    others = [rotate(v, "col", [(i, i ^ 1) for i in range(count)]) for v in sames]
    return sames + others


def chip_offsets():
    me = lax.axis_index("col")
    count = lax.axis_size("col")
    chip, core = me // 2, lax.rem(me, 2)
    chips = count // 2
    steps = (0, 1, 3, 2)
    return [2 * lax.rem(chip + chips - k, chips) + (core if same else 1 - core) for same in (True, False) for k in steps]


def from_stops_x(value):
    count = lax.axis_size("row")
    return [
        rotate(value, "row", [(i, i - i % X + (i + k) % X) for i in range(count)]) for k in (1, 3, 2)
    ]


def from_pair_z(value):
    count = lax.axis_size("row")
    return rotate(value, "row", [(i, i ^ X) for i in range(count)])


def from_pairs_z(value):
    count = lax.axis_size("row")
    return [rotate(value, "row", [(i, (i + 2 * X * k) % count) for i in range(count)]) for k in (1, 3, 2)]


def gather_kernel(*refs):
    pieces, (high_ref, low_ref, gram_ref, whole_ref) = refs[:-4], refs[-4:]
    height = pieces[0].shape[0]
    for piece, owner in zip(pieces, chip_offsets()):
        rows = pl.ds(pl.multiple_of(owner * height, height), height)
        value = piece[...]
        whole_ref[rows, :] = value
        high, low = halves(value)
        high_ref[rows, :] = high
        low_ref[rows, :] = low
    gram_ref[...] = dot(pieces[0][...], whole_ref[...], (1, 1))


def gather(pieces):
    height, rows = pieces[0].shape
    width = height * len(pieces)
    shapes = [(width, rows, BF16), (width, rows, BF16), (height, width, F32)]
    return pl.pallas_call(
        gather_kernel,
        out_shape=[jax.ShapeDtypeStruct((a, b), t) for a, b, t in shapes],
        scratch_shapes=[pltpu.VMEM((width, rows), F32)],
        cost_estimate=cost(4),
        compiler_params=room(16),
        name="gather",
    )(*pieces)


def turn_kernel(high_ref, low_ref, high_out, low_out):
    high_out[...] = high_ref[...].T
    low_out[...] = low_ref[...].T


def turn(high, low):
    width, rows = high.shape
    block = 512
    shape = pltpu.HBM((rows, width), BF16)
    return pl.pallas_call(
        turn_kernel,
        grid=(rows // block,),
        in_specs=[pl.BlockSpec((width, block), lambda i: (0, i))] * 2,
        out_specs=[pl.BlockSpec((block, width), lambda i: (i, 0))] * 2,
        out_shape=[shape, shape],
        cost_estimate=cost(3),
        compiler_params=room(8),
        name="turn",
    )(high, low)


def cross_kernel(high_ref, low_ref, trailing_ref, out_ref):
    @pl.when(pl.program_id(0) == 0)
    def _():
        out_ref[...] = jnp.zeros_like(out_ref)

    out_ref[...] += dot3((high_ref[...], low_ref[...]), halves(trailing_ref[...]))


def cross(high, low, trailing):
    width, rows = high.shape
    columns = trailing.shape[1]
    block = 512
    return pl.pallas_call(
        cross_kernel,
        grid=(rows // block,),
        in_specs=[
            pl.BlockSpec((width, block), lambda i: (0, i)),
            pl.BlockSpec((width, block), lambda i: (0, i)),
            pl.BlockSpec((block, columns), lambda i: (i, 0)),
        ],
        out_specs=pl.BlockSpec((width, columns), lambda i: (0, 0)),
        out_shape=jax.ShapeDtypeStruct((width, columns), F32),
        cost_estimate=cost(5),
        compiler_params=room(16),
        name="cross",
    )(high, low, trailing)


def group_kernel(own_ref, one_ref, three_ref, two_ref, prefix_ref, total_ref):
    place = lax.rem(lax.axis_index("row"), X)
    own, one, two, three = own_ref[...], one_ref[...], two_ref[...], three_ref[...]
    prefix_ref[...] = (
        own + jnp.where(place >= 1, one, 0.0) + jnp.where(place >= 2, two, 0.0) + jnp.where(place >= 3, three, 0.0)
    )
    total_ref[...] = (own + one) + (two + three)


def pair_kernel(before_ref, total_ref, other_ref, prefix_ref, pair_ref):
    odd = lax.rem(lax.div(lax.axis_index("row"), X), 2)
    other = other_ref[...]
    prefix_ref[...] = before_ref[...] + jnp.where(odd == 1, other, 0.0)
    pair_ref[...] = total_ref[...] + other


def pairs_kernel(before_ref, own_ref, one_ref, three_ref, two_ref, out_ref):
    place = lax.div(lax.axis_index("row"), 2 * X)
    own, one, two, three = own_ref[...], one_ref[...], two_ref[...], three_ref[...]
    out_ref[0] = (
        before_ref[...]
        + jnp.where(place >= 1, one, 0.0)
        + jnp.where(place >= 2, two, 0.0)
        + jnp.where(place >= 3, three, 0.0)
    )
    out_ref[1] = (own + one) + (two + three)


def small(kernel, shapes, *values):
    return pl.pallas_call(
        kernel,
        out_shape=[jax.ShapeDtypeStruct(shape, F32) for shape in shapes],
        cost_estimate=cost(1),
        compiler_params=room(2),
    )(*values)


def scan_kernel(pieces_ref, out_ref):
    stops, height, _ = pieces_ref.shape
    total = pieces_ref[0]
    out_ref[0, :height] = total
    for s in range(1, stops):
        total = total + pieces_ref[s]
        out_ref[s, :height] = total
    for s in range(stops):
        out_ref[s, height:] = total


def scan(pieces):
    stops, height, columns = pieces.shape
    return pl.pallas_call(
        scan_kernel,
        out_shape=jax.ShapeDtypeStruct((stops, 2 * height, columns), F32),
        cost_estimate=cost(1),
        compiler_params=room(4),
        name="scan",
    )(pieces)


def eliminate(matrices):
    order = matrices[0].shape[0]
    count = order // 8
    full = (8, order)
    lane = lax.broadcasted_iota(jnp.int32, full, 1)
    sublane = lax.broadcasted_iota(jnp.int32, full, 0)
    grids = [[m[8 * g : 8 * g + 8, :] for g in range(count)] for m in matrices]
    for p in range(count):
        start = 8 * p
        inside = (lane >= start) & (lane < start + 8)
        for grid in grids:
            block = grid[p]
            columns = [jnp.broadcast_to(block[:, start + c : start + c + 1], full) for c in range(8)]
            entry = [[None] * r + [jnp.broadcast_to(columns[r][c : c + 1, :], full) for c in range(r, 8)] for r in range(8)]
            rows = [jnp.broadcast_to(block[r : r + 1, :], full) for r in range(8)]
            rows = [jnp.where(inside, jnp.where(lane == start + r, 1.0, 0.0), rows[r]) for r in range(8)]
            inverse, multiple = [], [[None] * 8 for _ in range(8)]
            for k in range(8):
                inverse.append(1.0 / entry[k][k])
                for r in range(k + 1, 8):
                    multiple[r][k] = entry[k][r] * inverse[k]
                for r in range(k + 1, 8):
                    for c in range(r, 8):
                        entry[r][c] = entry[r][c] - multiple[r][k] * entry[k][c]
                    rows[r] = rows[r] - multiple[r][k] * rows[k]
            result = rows[0]
            for r in range(1, 8):
                result = jnp.where(sublane == r, rows[r], result)
            for c in range(8):
                column = entry[0][c]
                for r in range(1, c + 1):
                    column = jnp.where(sublane == r, entry[r][c], column)
                result = jnp.where((lane == start + c) & (sublane <= c), column, result)
            if p < count - 1:
                solved = [rows[k] * inverse[k] for k in range(8)]
                for k in range(6, -1, -1):
                    for r in range(k + 1, 8):
                        solved[k] = solved[k] - multiple[r][k] * solved[r]
                for g in range(p + 1, count):
                    value = jnp.where(inside, 0.0, grid[g])
                    for k in range(8):
                        value = value - jnp.broadcast_to(grid[g][:, start + k : start + k + 1], full) * solved[k]
                    grid[g] = value
            grid[p] = result
    return [jnp.concatenate(grid, 0) for grid in grids]


def split(reduced):
    order = reduced.shape[0]
    row = lax.broadcasted_iota(jnp.int32, (order, order), 0)
    column = lax.broadcasted_iota(jnp.int32, (order, order), 1)
    pivots = jnp.sum(jnp.where(row == column, reduced, 0.0), axis=1, keepdims=True)
    scale = lax.rsqrt(pivots)
    upper = jnp.where(row <= column, reduced, 0.0) * scale
    lower = jnp.where(row > column, reduced, jnp.where(row == column, 1.0, 0.0)) * scale
    return upper, lower


def factor_kernel(*refs):
    pieces, (upper_ref, high_ref, low_ref, gram_ref, inverse_ref) = refs[:-5], refs[-5:]
    count, height, order = pieces[0].shape
    half = order // 2
    for piece, owner in zip(pieces, chip_offsets()):
        gram_ref[:, pl.ds(pl.multiple_of(owner * height, height), height), :] = piece[...]
    tops = eliminate([gram_ref[i, :half, :half] for i in range(count)])
    schurs, sides = [], []
    for i, reduced in enumerate(tops):
        upper, inverse = split(reduced)
        across = dot(inverse, gram_ref[i, :half, half:])
        side = dot(gram_ref[i, half:, :half], inverse, (1, 1))
        schurs.append(gram_ref[i, half:, half:] - dot(side, across))
        sides.append(dot(side, inverse))
        if i == 0:
            upper_ref[:half, :half] = upper
            upper_ref[:half, half:] = across
            upper_ref[half:, :half] = jnp.zeros((half, half), F32)
        inverse_ref[i, :half, :half] = inverse
        inverse_ref[i, :half, half:] = jnp.zeros((half, half), F32)
    for i, reduced in enumerate(eliminate(schurs)):
        upper, inverse = split(reduced)
        if i == 0:
            upper_ref[half:, half:] = upper
        inverse_ref[i, half:, half:] = inverse
        inverse_ref[i, half:, :half] = -dot(inverse, sides[i])
    high_ref[0], low_ref[0] = halves(inverse_ref[0])
    last = inverse_ref[1]
    high_ref[1], low_ref[1] = halves(dot(last, last, (0, 0)))


def factor(pieces):
    count, _, order = pieces[0].shape
    return pl.pallas_call(
        factor_kernel,
        out_shape=[
            jax.ShapeDtypeStruct((order, order), F32),
            pltpu.HBM((count, order, order), BF16),
            pltpu.HBM((count, order, order), BF16),
        ],
        scratch_shapes=[pltpu.VMEM((count, order, order), F32)] * 2,
        cost_estimate=cost(16),
        compiler_params=room(8),
        name="factor",
    )(*pieces)


def project_kernel(sh_ref, sl_ref, sums_ref, high_ref, low_ref, trailing_ref, blocks_ref, out_ref, ch_ref, cl_ref):
    stops, both, columns = sums_ref.shape
    height = both // 2

    @pl.when(pl.program_id(0) == 0)
    def _():
        total = sums_ref[:, height:, :].reshape(stops * height, columns)
        high, low = halves(dot3((sh_ref[1], sl_ref[1]), halves(total)))
        ch_ref[...] = high
        cl_ref[...] = low
        prefix = sums_ref[:, :height, :].reshape(stops * height, columns)
        blocks_ref[...] = dot3((sh_ref[0], sl_ref[0]), halves(prefix))

    out_ref[...] = trailing_ref[...] - dot3((high_ref[...], low_ref[...]), (ch_ref[...], cl_ref[...]))


def in_hbm(value):
    return pltpu.with_memory_space_constraint(value, pltpu.HBM)


def project(solves, sums, high, low, trailing):
    rows, columns = trailing.shape
    width = high.shape[1]
    block = 256
    whole = pl.BlockSpec(solves[0].shape, lambda i: (0, 0, 0))
    return pl.pallas_call(
        project_kernel,
        grid=(rows // block,),
        in_specs=[
            whole,
            whole,
            pl.BlockSpec(sums.shape, lambda i: (0, 0, 0)),
            pl.BlockSpec((block, width), lambda i: (i, 0)),
            pl.BlockSpec((block, width), lambda i: (i, 0)),
            pl.BlockSpec((block, columns), lambda i: (i, 0)),
        ],
        out_specs=[
            pl.BlockSpec((width, columns), lambda i: (0, 0)),
            pl.BlockSpec((block, columns), lambda i: (i, 0)),
        ],
        out_shape=[
            jax.ShapeDtypeStruct((width, columns), F32),
            jax.ShapeDtypeStruct((rows, columns), F32),
        ],
        scratch_shapes=[pltpu.VMEM((width, columns), BF16)] * 2,
        cost_estimate=cost(8),
        compiler_params=room(16),
        name="project",
    )(*[in_hbm(s) for s in solves], sums, in_hbm(high), in_hbm(low), in_hbm(trailing))


def stages(panel_transposed, trailing):
    stops = lax.axis_size("row")
    high, low, own_gram = gather(from_chips(panel_transposed))
    width = high.shape[0]
    columns = trailing.shape[1]
    piece = own_gram.shape

    def exchange(value):
        return lax.all_to_all(value, "row", 0, 0, tiled=True)

    behind = from_stops_x(own_gram)
    own_cross = cross(high, low, trailing)
    pieces = exchange(own_cross.reshape(stops, width // stops, columns))

    prefix, total = small(group_kernel, [piece] * 2, own_gram, *behind)
    other = from_pair_z(total)
    prefix, total = small(pair_kernel, [piece] * 2, prefix, total, other)
    behind = from_pairs_z(total)
    (grams,) = small(pairs_kernel, [(2,) + piece], prefix, total, *behind)
    grams = from_chips(grams)
    high, low = turn(high, low)

    both = scan(pieces)
    sums = exchange(both)
    grams, both = lax.optimization_barrier((grams, both))
    stop_factors, *solves = factor(grams)
    stop_blocks, projected = project(solves, sums, high, low, trailing)
    return (stop_factors, stop_blocks, projected)


def solution(mesh):
    return jax.shard_map(
        stages,
        mesh=mesh,
        in_specs=(P("col", "row"), P("row", "col")),
        out_specs=(P("row", None), P("row", "col"), P("row", "col")),
        check_vma=False,
    )
```

```python
import jax
import jax.numpy as jnp
from jax import lax
from jax.experimental import pallas as pl
from jax.experimental.pallas import tpu as pltpu
from jax.sharding import PartitionSpec as P


HIGHEST = lax.Precision.HIGHEST
F32 = jnp.float32
BF16 = jnp.bfloat16
X = 4


def dot(left, right, dims=(1, 0), precision=HIGHEST):
    return lax.dot_general(
        left,
        right,
        (((dims[0],), (dims[1],)), ((), ())),
        precision=precision,
        preferred_element_type=F32,
    )


def halves(value):
    high = value.astype(BF16)
    return high, (value - high.astype(F32)).astype(BF16)


def dot3(left, right, dims=(1, 0)):
    (lh, ll), (rh, rl) = left, right
    default = lax.Precision.DEFAULT
    return dot(lh, rh, dims, default) + (dot(ll, rh, dims, default) + dot(lh, rl, dims, default))


def room(mebibytes):
    return pltpu.CompilerParams(vmem_limit_bytes=mebibytes * 2**20)


def cost(us):
    return pl.CostEstimate(flops=int(us * 5e8), bytes_accessed=int(us * 1e6), transcendentals=0)


def in_hbm(value):
    return pltpu.with_memory_space_constraint(value, pltpu.HBM)


def rotate(value, axis, pairs):
    return lax.ppermute(value, axis, pairs)


def from_chips(value):
    count = lax.axis_size("col")
    sames = [value] + [
        rotate(value, "col", [(i, (i + 2 * k) % count) for i in range(count)]) for k in (1, 3, 2)
    ]
    others = [rotate(v, "col", [(i, i ^ 1) for i in range(count)]) for v in sames]
    return sames + others


def chip_offsets():
    me = lax.axis_index("col")
    count = lax.axis_size("col")
    chip, core = me // 2, lax.rem(me, 2)
    chips = count // 2
    steps = (0, 1, 3, 2)
    return [2 * lax.rem(chip + chips - k, chips) + (core if same else 1 - core) for same in (True, False) for k in steps]


def from_stops_x(value):
    count = lax.axis_size("row")
    return [
        rotate(value, "row", [(i, i - i % X + (i + k) % X) for i in range(count)]) for k in (1, 3, 2)
    ]


def from_pair_z(value):
    count = lax.axis_size("row")
    return rotate(value, "row", [(i, i ^ X) for i in range(count)])


def from_pairs_z(value):
    count = lax.axis_size("row")
    return [rotate(value, "row", [(i, (i + 2 * X * k) % count) for i in range(count)]) for k in (1, 3, 2)]


def gather_kernel(panel_ref, *refs):
    pieces, (high_ref, low_ref, gram_ref, whole_ref, own_ref, arrived) = refs[:-6], refs[-6:]
    height = own_ref.shape[0]
    fetch = pltpu.make_async_copy(panel_ref, own_ref, arrived)
    fetch.start()
    owners = chip_offsets()

    def place(value, owner):
        rows = pl.ds(pl.multiple_of(owner * height, height), height)
        whole_ref[rows, :] = value
        high, low = halves(value)
        high_ref[rows, :] = high
        low_ref[rows, :] = low

    for piece, owner in zip(pieces, owners[1:]):
        place(piece[...], owner)
    fetch.wait()
    place(own_ref[...], owners[0])
    gram_ref[...] = dot(own_ref[...], whole_ref[...], (1, 1))


def gather(pieces):
    height, rows = pieces[0].shape
    width = height * len(pieces)
    shapes = [(width, rows, BF16), (width, rows, BF16), (height, width, F32)]
    return pl.pallas_call(
        gather_kernel,
        in_specs=[pl.BlockSpec(memory_space=pl.ANY)] + [pl.BlockSpec(memory_space=pltpu.VMEM)] * (len(pieces) - 1),
        out_shape=[jax.ShapeDtypeStruct((a, b), t) for a, b, t in shapes],
        scratch_shapes=[pltpu.VMEM((width, rows), F32), pltpu.VMEM((height, rows), F32), pltpu.SemaphoreType.DMA],
        cost_estimate=cost(4),
        compiler_params=room(16),
        name="gather",
    )(in_hbm(pieces[0]), *pieces[1:])


def turn_kernel(high_ref, low_ref, high_out, low_out):
    high_out[...] = high_ref[...].T
    low_out[...] = low_ref[...].T


def turn(high, low):
    width, rows = high.shape
    block = 512
    shape = pltpu.HBM((rows, width), BF16)
    return pl.pallas_call(
        turn_kernel,
        grid=(rows // block,),
        in_specs=[pl.BlockSpec((width, block), lambda i: (0, i))] * 2,
        out_specs=[pl.BlockSpec((block, width), lambda i: (i, 0))] * 2,
        out_shape=[shape, shape],
        cost_estimate=cost(3),
        compiler_params=room(8),
        name="turn",
    )(high, low)


def halve_kernel(value_ref, high_ref, low_ref):
    high_ref[...], low_ref[...] = halves(value_ref[...])


def halve(value):
    rows, columns = value.shape
    block = 256
    spec = pl.BlockSpec((block, columns), lambda i: (i, 0))
    shape = jax.ShapeDtypeStruct(value.shape, BF16)
    return pl.pallas_call(
        halve_kernel,
        grid=(rows // block,),
        in_specs=[spec],
        out_specs=[spec] * 2,
        out_shape=[shape] * 2,
        cost_estimate=cost(2),
        compiler_params=room(8),
        name="halve",
    )(in_hbm(value))


def cross_kernel(high_ref, low_ref, right_high_ref, right_low_ref, out_ref):
    product = dot3((high_ref[...], low_ref[...]), (right_high_ref[...], right_low_ref[...]))

    @pl.when(pl.program_id(0) == 0)
    def _():
        out_ref[...] = product

    @pl.when(pl.program_id(0) > 0)
    def _():
        out_ref[...] += product


def cross(high, low, right_high, right_low):
    width, rows = high.shape
    columns = right_high.shape[1]
    block = 1024
    left = pl.BlockSpec((width, block), lambda i: (0, i))
    right = pl.BlockSpec((block, columns), lambda i: (i, 0))
    return pl.pallas_call(
        cross_kernel,
        grid=(rows // block,),
        in_specs=[left, left, right, right],
        out_specs=pl.BlockSpec((width, columns), lambda i: (0, 0)),
        out_shape=jax.ShapeDtypeStruct((width, columns), F32),
        cost_estimate=cost(4),
        compiler_params=room(16),
        name="cross",
    )(high, low, right_high, right_low)


def group_kernel(own_ref, one_ref, three_ref, two_ref, prefix_ref, total_ref):
    place = lax.rem(lax.axis_index("row"), X)
    own, one, two, three = own_ref[...], one_ref[...], two_ref[...], three_ref[...]
    prefix_ref[...] = (
        own + jnp.where(place >= 1, one, 0.0) + jnp.where(place >= 2, two, 0.0) + jnp.where(place >= 3, three, 0.0)
    )
    total_ref[...] = (own + one) + (two + three)


def pair_kernel(before_ref, total_ref, other_ref, prefix_ref, pair_ref):
    odd = lax.rem(lax.div(lax.axis_index("row"), X), 2)
    other = other_ref[...]
    prefix_ref[...] = before_ref[...] + jnp.where(odd == 1, other, 0.0)
    pair_ref[...] = total_ref[...] + other


def pairs_kernel(before_ref, own_ref, one_ref, three_ref, two_ref, out_ref):
    place = lax.div(lax.axis_index("row"), 2 * X)
    own, one, two, three = own_ref[...], one_ref[...], two_ref[...], three_ref[...]
    out_ref[0] = (
        before_ref[...]
        + jnp.where(place >= 1, one, 0.0)
        + jnp.where(place >= 2, two, 0.0)
        + jnp.where(place >= 3, three, 0.0)
    )
    out_ref[1] = (own + one) + (two + three)


def small(kernel, shapes, *values):
    return pl.pallas_call(
        kernel,
        out_shape=[jax.ShapeDtypeStruct(shape, F32) for shape in shapes],
        cost_estimate=cost(1),
        compiler_params=room(2),
    )(*values)


def scan_kernel(pieces_ref, out_ref):
    stops, height, _ = pieces_ref.shape
    total = pieces_ref[0]
    out_ref[0, :height] = total
    for s in range(1, stops):
        total = total + pieces_ref[s]
        out_ref[s, :height] = total
    for s in range(stops):
        out_ref[s, height:] = total


def scan(pieces):
    stops, height, columns = pieces.shape
    return pl.pallas_call(
        scan_kernel,
        out_shape=jax.ShapeDtypeStruct((stops, 2 * height, columns), F32),
        cost_estimate=cost(1),
        compiler_params=room(4),
        name="scan",
    )(pieces)


def eliminate(matrices):
    order = matrices[0].shape[0]
    count = order // 8
    full = (8, order)
    lane = lax.broadcasted_iota(jnp.int32, full, 1)
    sublane = lax.broadcasted_iota(jnp.int32, full, 0)
    grids = [[m[8 * g : 8 * g + 8, :] for g in range(count)] for m in matrices]
    for p in range(count):
        start = 8 * p
        inside = (lane >= start) & (lane < start + 8)
        for grid in grids:
            block = grid[p]
            columns = [jnp.broadcast_to(block[:, start + c : start + c + 1], full) for c in range(8)]
            entry = [[None] * r + [jnp.broadcast_to(columns[r][c : c + 1, :], full) for c in range(r, 8)] for r in range(8)]
            rows = [jnp.broadcast_to(block[r : r + 1, :], full) for r in range(8)]
            rows = [jnp.where(inside, jnp.where(lane == start + r, 1.0, 0.0), rows[r]) for r in range(8)]
            inverse, multiple = [], [[None] * 8 for _ in range(8)]
            for k in range(8):
                inverse.append(1.0 / entry[k][k])
                for r in range(k + 1, 8):
                    multiple[r][k] = entry[k][r] * inverse[k]
                for r in range(k + 1, 8):
                    for c in range(r, 8):
                        entry[r][c] = entry[r][c] - multiple[r][k] * entry[k][c]
                    rows[r] = rows[r] - multiple[r][k] * rows[k]
            result = rows[0]
            for r in range(1, 8):
                result = jnp.where(sublane == r, rows[r], result)
            for c in range(8):
                column = entry[0][c]
                for r in range(1, c + 1):
                    column = jnp.where(sublane == r, entry[r][c], column)
                result = jnp.where((lane == start + c) & (sublane <= c), column, result)
            if p < count - 1:
                solved = [rows[k] * inverse[k] for k in range(8)]
                for k in range(6, -1, -1):
                    for r in range(k + 1, 8):
                        solved[k] = solved[k] - multiple[r][k] * solved[r]
                for g in range(p + 1, count):
                    value = jnp.where(inside, 0.0, grid[g])
                    for k in range(8):
                        value = value - jnp.broadcast_to(grid[g][:, start + k : start + k + 1], full) * solved[k]
                    grid[g] = value
            grid[p] = result
    return [jnp.concatenate(grid, 0) for grid in grids]


def split(reduced):
    order = reduced.shape[0]
    row = lax.broadcasted_iota(jnp.int32, (order, order), 0)
    column = lax.broadcasted_iota(jnp.int32, (order, order), 1)
    pivots = jnp.sum(jnp.where(row == column, reduced, 0.0), axis=1, keepdims=True)
    scale = lax.rsqrt(pivots)
    upper = jnp.where(row <= column, reduced, 0.0) * scale
    lower = jnp.where(row > column, reduced, jnp.where(row == column, 1.0, 0.0)) * scale
    return upper, lower


def factor_kernel(*refs):
    pieces, (upper_ref, high_ref, low_ref, gram_ref, inverse_ref) = refs[:-5], refs[-5:]
    count, height, order = pieces[0].shape
    half = order // 2
    for piece, owner in zip(pieces, chip_offsets()):
        gram_ref[:, pl.ds(pl.multiple_of(owner * height, height), height), :] = piece[...]
    tops = eliminate([gram_ref[i, :half, :half] for i in range(count)])
    schurs, sides = [], []
    for i, reduced in enumerate(tops):
        upper, inverse = split(reduced)
        across = dot(inverse, gram_ref[i, :half, half:])
        side = dot(gram_ref[i, half:, :half], inverse, (1, 1))
        schurs.append(gram_ref[i, half:, half:] - dot(side, across))
        sides.append(dot(side, inverse))
        if i == 0:
            upper_ref[:half, :half] = upper
            upper_ref[:half, half:] = across
            upper_ref[half:, :half] = jnp.zeros((half, half), F32)
        inverse_ref[i, :half, :half] = inverse
        inverse_ref[i, :half, half:] = jnp.zeros((half, half), F32)
    for i, reduced in enumerate(eliminate(schurs)):
        upper, inverse = split(reduced)
        if i == 0:
            upper_ref[half:, half:] = upper
        inverse_ref[i, half:, half:] = inverse
        inverse_ref[i, half:, :half] = -dot(inverse, sides[i])
    high_ref[0], low_ref[0] = halves(inverse_ref[0])
    last = inverse_ref[1]
    high_ref[1], low_ref[1] = halves(dot(last, last, (0, 0)))


def factor(pieces):
    count, _, order = pieces[0].shape
    return pl.pallas_call(
        factor_kernel,
        out_shape=[
            jax.ShapeDtypeStruct((order, order), F32),
            pltpu.HBM((count, order, order), BF16),
            pltpu.HBM((count, order, order), BF16),
        ],
        scratch_shapes=[pltpu.VMEM((count, order, order), F32)] * 2,
        cost_estimate=cost(16),
        compiler_params=room(8),
        name="factor",
    )(*pieces)


def project_kernel(sums_ref, *refs):
    (sh_from, sl_from, high_from, low_from, trailing_from, blocks_to, out_to), refs = refs[:7], refs[7:]
    sh_ref, sl_ref, high_ref, low_ref, trailing_ref, blocks_ref, out_ref, first, coming, going = refs
    stops, both, columns = sums_ref.shape
    height = both // 2
    rows = trailing_ref.shape[0]
    chunks = coming.shape[0]
    size = rows // chunks
    solves = [
        pltpu.make_async_copy(sh_from, sh_ref, first.at[0]),
        pltpu.make_async_copy(sl_from, sl_ref, first.at[1]),
    ]
    for copy in solves:
        copy.start()
    arrivals = []
    for i in range(chunks):
        part = pl.ds(i * size, size)
        arrivals.append(
            [
                pltpu.make_async_copy(source.at[part], target.at[part], coming.at[i, k])
                for k, (source, target) in enumerate(
                    ((high_from, high_ref), (low_from, low_ref), (trailing_from, trailing_ref))
                )
            ]
        )
        for copy in arrivals[-1]:
            copy.start()
    total = halves(sums_ref[:, height:, :].reshape(stops * height, columns))
    prefix = halves(sums_ref[:, :height, :].reshape(stops * height, columns))
    for copy in solves:
        copy.wait()
    coeffs = halves(dot3((sh_ref[1], sl_ref[1]), total))
    blocks_ref[...] = dot3((sh_ref[0], sl_ref[0]), prefix)
    leaving = [pltpu.make_async_copy(blocks_ref, blocks_to, going.at[chunks])]
    leaving[0].start()
    for i in range(chunks):
        part = pl.ds(i * size, size)
        for copy in arrivals[i]:
            copy.wait()
        out_ref[part, :] = trailing_ref[part, :] - dot3((high_ref[part, :], low_ref[part, :]), coeffs)
        leaving.append(pltpu.make_async_copy(out_ref.at[part], out_to.at[part], going.at[i]))
        leaving[-1].start()
    for copy in leaving:
        copy.wait()


def project(solves, sums, high, low, trailing):
    rows, columns = trailing.shape
    width = high.shape[1]
    chunks = 8
    anywhere = pl.BlockSpec(memory_space=pl.ANY)
    return pl.pallas_call(
        project_kernel,
        in_specs=[pl.BlockSpec(memory_space=pltpu.VMEM)] + [anywhere] * 5,
        out_specs=[anywhere] * 2,
        out_shape=[pltpu.HBM((width, columns), F32), pltpu.HBM((rows, columns), F32)],
        scratch_shapes=[pltpu.VMEM(s.shape, BF16) for s in (*solves, high, low)]
        + [
            pltpu.VMEM((rows, columns), F32),
            pltpu.VMEM((width, columns), F32),
            pltpu.VMEM((rows, columns), F32),
            pltpu.SemaphoreType.DMA((2,)),
            pltpu.SemaphoreType.DMA((chunks, 3)),
            pltpu.SemaphoreType.DMA((chunks + 1,)),
        ],
        cost_estimate=cost(6),
        compiler_params=room(24),
        name="project",
    )(sums, *[in_hbm(v) for v in (*solves, high, low, trailing)])


def stages(panel_transposed, trailing):
    stops = lax.axis_size("row")
    high, low, own_gram = gather(from_chips(panel_transposed))
    width = high.shape[0]
    columns = trailing.shape[1]
    piece = own_gram.shape

    def exchange(value):
        return lax.all_to_all(value, "row", 0, 0, tiled=True)

    behind = from_stops_x(own_gram)
    own_cross = cross(high, low, *halve(trailing))
    pieces = exchange(own_cross.reshape(stops, width // stops, columns))

    prefix, total = small(group_kernel, [piece] * 2, own_gram, *behind)
    other = from_pair_z(total)
    prefix, total = small(pair_kernel, [piece] * 2, prefix, total, other)
    behind = from_pairs_z(total)
    (grams,) = small(pairs_kernel, [(2,) + piece], prefix, total, *behind)
    grams = from_chips(grams)
    high, low = turn(high, low)

    both = scan(pieces)
    sums = exchange(both)
    grams, both = lax.optimization_barrier((grams, both))
    stop_factors, *solves = factor(grams)
    stop_blocks, projected = project(solves, sums, high, low, trailing)
    return (stop_factors, stop_blocks, projected)


def solution(mesh):
    return jax.shard_map(
        stages,
        mesh=mesh,
        in_specs=(P("col", "row"), P("row", "col")),
        out_specs=(P("row", None), P("row", "col"), P("row", "col")),
        check_vma=False,
    )
```

```python
import jax
import jax.numpy as jnp
from jax import lax
from jax.experimental import pallas as pl
from jax.experimental.pallas import tpu as pltpu
from jax.sharding import PartitionSpec as P


HIGHEST = lax.Precision.HIGHEST
F32 = jnp.float32
BF16 = jnp.bfloat16
X = 4


def dot(left, right, dims=(1, 0), precision=HIGHEST):
    return lax.dot_general(
        left,
        right,
        (((dims[0],), (dims[1],)), ((), ())),
        precision=precision,
        preferred_element_type=F32,
    )


def halves(value):
    high = value.astype(BF16)
    return high, (value - high.astype(F32)).astype(BF16)


def dot3(left, right, dims=(1, 0)):
    (lh, ll), (rh, rl) = left, right
    default = lax.Precision.DEFAULT
    return dot(lh, rh, dims, default) + (dot(ll, rh, dims, default) + dot(lh, rl, dims, default))


def dot4(left, right, dims=(1, 0)):
    return dot3(left, right, dims) + dot(left[1], right[1], dims, lax.Precision.DEFAULT)


def room(mebibytes):
    return pltpu.CompilerParams(vmem_limit_bytes=mebibytes * 2**20)


def cost(us):
    return pl.CostEstimate(flops=int(us * 5e8), bytes_accessed=int(us * 1e6), transcendentals=0)


def in_hbm(value):
    return pltpu.with_memory_space_constraint(value, pltpu.HBM)


def rotate(value, axis, pairs):
    return lax.ppermute(value, axis, pairs)


def from_chips(value):
    count = lax.axis_size("col")
    sames = [value] + [
        rotate(value, "col", [(i, (i + 2 * k) % count) for i in range(count)]) for k in (1, 3, 2)
    ]
    others = [rotate(v, "col", [(i, i ^ 1) for i in range(count)]) for v in sames]
    return sames + others


def chip_offsets():
    me = lax.axis_index("col")
    count = lax.axis_size("col")
    chip, core = me // 2, lax.rem(me, 2)
    chips = count // 2
    steps = (0, 1, 3, 2)
    return [2 * lax.rem(chip + chips - k, chips) + (core if same else 1 - core) for same in (True, False) for k in steps]


def from_stops_x(value):
    count = lax.axis_size("row")
    return [
        rotate(value, "row", [(i, i - i % X + (i + k) % X) for i in range(count)]) for k in (1, 3, 2)
    ]


def from_pair_z(value):
    count = lax.axis_size("row")
    return rotate(value, "row", [(i, i ^ X) for i in range(count)])


def from_pairs_z(value):
    count = lax.axis_size("row")
    return [rotate(value, "row", [(i, (i + 2 * X * k) % count) for i in range(count)]) for k in (1, 3, 2)]


def gather_kernel(panel_ref, *refs):
    pieces, (high_ref, low_ref, gram_ref, own_ref, arrived) = refs[:-5], refs[-5:]
    height = own_ref.shape[0]
    fetch = pltpu.make_async_copy(panel_ref, own_ref, arrived)
    fetch.start()
    owners = chip_offsets()

    def place(value, owner):
        rows = pl.ds(pl.multiple_of(owner * height, height), height)
        high, low = halves(value)
        high_ref[rows, :] = high
        low_ref[rows, :] = low

    for piece, owner in zip(pieces, owners[1:]):
        place(piece[...], owner)
    fetch.wait()
    place(own_ref[...], owners[0])
    gram_ref[...] = dot4(halves(own_ref[...]), (high_ref[...], low_ref[...]), (1, 1))


def gather(pieces):
    height, rows = pieces[0].shape
    width = height * len(pieces)
    shapes = [(width, rows, BF16), (width, rows, BF16), (height, width, F32)]
    return pl.pallas_call(
        gather_kernel,
        in_specs=[pl.BlockSpec(memory_space=pl.ANY)] + [pl.BlockSpec(memory_space=pltpu.VMEM)] * (len(pieces) - 1),
        out_shape=[jax.ShapeDtypeStruct((a, b), t) for a, b, t in shapes],
        scratch_shapes=[pltpu.VMEM((height, rows), F32), pltpu.SemaphoreType.DMA],
        cost_estimate=cost(4),
        compiler_params=room(16),
        name="gather",
    )(in_hbm(pieces[0]), *pieces[1:])


def turn_kernel(high_ref, low_ref, high_out, low_out):
    high_out[...] = high_ref[...].T
    low_out[...] = low_ref[...].T


def turn(high, low):
    width, rows = high.shape
    block = 512
    shape = pltpu.HBM((rows, width), BF16)
    return pl.pallas_call(
        turn_kernel,
        grid=(rows // block,),
        in_specs=[pl.BlockSpec((width, block), lambda i: (0, i))] * 2,
        out_specs=[pl.BlockSpec((block, width), lambda i: (i, 0))] * 2,
        out_shape=[shape, shape],
        cost_estimate=cost(3),
        compiler_params=room(8),
        name="turn",
    )(high, low)


def halve_kernel(value_ref, high_ref, low_ref):
    high_ref[...], low_ref[...] = halves(value_ref[...])


def halve(value):
    rows, columns = value.shape
    block = 256
    spec = pl.BlockSpec((block, columns), lambda i: (i, 0))
    shape = jax.ShapeDtypeStruct(value.shape, BF16)
    return pl.pallas_call(
        halve_kernel,
        grid=(rows // block,),
        in_specs=[spec],
        out_specs=[spec] * 2,
        out_shape=[shape] * 2,
        cost_estimate=cost(2),
        compiler_params=room(8),
        name="halve",
    )(in_hbm(value))


def cross_kernel(high_ref, low_ref, right_high_ref, right_low_ref, out_ref):
    out_ref[...] = dot3((high_ref[...], low_ref[...]), (right_high_ref[...], right_low_ref[...]))


def cross(high, low, right_high, right_low):
    return pl.pallas_call(
        cross_kernel,
        out_shape=jax.ShapeDtypeStruct((high.shape[0], right_high.shape[1]), F32),
        cost_estimate=cost(4),
        compiler_params=room(16),
        name="cross",
    )(high, low, right_high, right_low)


def group_kernel(own_ref, one_ref, three_ref, two_ref, prefix_ref, total_ref):
    place = lax.rem(lax.axis_index("row"), X)
    own, one, two, three = own_ref[...], one_ref[...], two_ref[...], three_ref[...]
    prefix_ref[...] = (
        own + jnp.where(place >= 1, one, 0.0) + jnp.where(place >= 2, two, 0.0) + jnp.where(place >= 3, three, 0.0)
    )
    total_ref[...] = (own + one) + (two + three)


def pair_kernel(before_ref, total_ref, other_ref, prefix_ref, pair_ref):
    odd = lax.rem(lax.div(lax.axis_index("row"), X), 2)
    other = other_ref[...]
    prefix_ref[...] = before_ref[...] + jnp.where(odd == 1, other, 0.0)
    pair_ref[...] = total_ref[...] + other


def pairs_kernel(before_ref, own_ref, one_ref, three_ref, two_ref, out_ref):
    place = lax.div(lax.axis_index("row"), 2 * X)
    own, one, two, three = own_ref[...], one_ref[...], two_ref[...], three_ref[...]
    out_ref[0] = (
        before_ref[...]
        + jnp.where(place >= 1, one, 0.0)
        + jnp.where(place >= 2, two, 0.0)
        + jnp.where(place >= 3, three, 0.0)
    )
    out_ref[1] = (own + one) + (two + three)


def small(kernel, shapes, *values):
    return pl.pallas_call(
        kernel,
        out_shape=[jax.ShapeDtypeStruct(shape, F32) for shape in shapes],
        cost_estimate=cost(1),
        compiler_params=room(2),
    )(*values)


def scan_kernel(pieces_ref, out_ref):
    stops, height, _ = pieces_ref.shape
    total = pieces_ref[0]
    out_ref[0, :height] = total
    for s in range(1, stops):
        total = total + pieces_ref[s]
        out_ref[s, :height] = total
    for s in range(stops):
        out_ref[s, height:] = total


def scan(pieces):
    stops, height, columns = pieces.shape
    return pl.pallas_call(
        scan_kernel,
        out_shape=jax.ShapeDtypeStruct((stops, 2 * height, columns), F32),
        cost_estimate=cost(1),
        compiler_params=room(4),
        name="scan",
    )(pieces)


def eliminate(matrices):
    order = matrices[0].shape[0]
    count = order // 8
    full = (8, order)
    lane = lax.broadcasted_iota(jnp.int32, full, 1)
    sublane = lax.broadcasted_iota(jnp.int32, full, 0)
    grids = [[m[8 * g : 8 * g + 8, :] for g in range(count)] for m in matrices]
    for p in range(count):
        start = 8 * p
        inside = (lane >= start) & (lane < start + 8)
        for grid in grids:
            block = grid[p]
            columns = [jnp.broadcast_to(block[:, start + c : start + c + 1], full) for c in range(8)]
            entry = [[None] * r + [jnp.broadcast_to(columns[r][c : c + 1, :], full) for c in range(r, 8)] for r in range(8)]
            rows = [jnp.broadcast_to(block[r : r + 1, :], full) for r in range(8)]
            rows = [jnp.where(inside, jnp.where(lane == start + r, 1.0, 0.0), rows[r]) for r in range(8)]
            inverse, multiple = [], [[None] * 8 for _ in range(8)]
            for k in range(8):
                inverse.append(1.0 / entry[k][k])
                for r in range(k + 1, 8):
                    multiple[r][k] = entry[k][r] * inverse[k]
                for r in range(k + 1, 8):
                    for c in range(r, 8):
                        entry[r][c] = entry[r][c] - multiple[r][k] * entry[k][c]
                    rows[r] = rows[r] - multiple[r][k] * rows[k]
            result = rows[0]
            for r in range(1, 8):
                result = jnp.where(sublane == r, rows[r], result)
            for c in range(8):
                column = entry[0][c]
                for r in range(1, c + 1):
                    column = jnp.where(sublane == r, entry[r][c], column)
                result = jnp.where((lane == start + c) & (sublane <= c), column, result)
            if p < count - 1:
                solved = [rows[k] * inverse[k] for k in range(8)]
                for k in range(6, -1, -1):
                    for r in range(k + 1, 8):
                        solved[k] = solved[k] - multiple[r][k] * solved[r]
                for g in range(p + 1, count):
                    value = jnp.where(inside, 0.0, grid[g])
                    for k in range(8):
                        value = value - jnp.broadcast_to(grid[g][:, start + k : start + k + 1], full) * solved[k]
                    grid[g] = value
            grid[p] = result
    return [jnp.concatenate(grid, 0) for grid in grids]


def split(reduced):
    order = reduced.shape[0]
    row = lax.broadcasted_iota(jnp.int32, (order, order), 0)
    column = lax.broadcasted_iota(jnp.int32, (order, order), 1)
    pivots = jnp.sum(jnp.where(row == column, reduced, 0.0), axis=1, keepdims=True)
    scale = lax.rsqrt(pivots)
    upper = jnp.where(row <= column, reduced, 0.0) * scale
    lower = jnp.where(row > column, reduced, jnp.where(row == column, 1.0, 0.0)) * scale
    return upper, lower


def factor_kernel(*refs):
    pieces, (upper_ref, high_ref, low_ref, gram_ref, inverse_ref) = refs[:-5], refs[-5:]
    count, height, order = pieces[0].shape
    half = order // 2
    for piece, owner in zip(pieces, chip_offsets()):
        gram_ref[:, pl.ds(pl.multiple_of(owner * height, height), height), :] = piece[...]
    tops = eliminate([gram_ref[i, :half, :half] for i in range(count)])
    schurs, sides = [], []
    for i, reduced in enumerate(tops):
        upper, inverse = split(reduced)
        across = dot(inverse, gram_ref[i, :half, half:])
        side = dot(gram_ref[i, half:, :half], inverse, (1, 1))
        schurs.append(gram_ref[i, half:, half:] - dot(side, across))
        sides.append(dot(side, inverse))
        if i == 0:
            upper_ref[:half, :half] = upper
            upper_ref[:half, half:] = across
            upper_ref[half:, :half] = jnp.zeros((half, half), F32)
        inverse_ref[i, :half, :half] = inverse
        inverse_ref[i, :half, half:] = jnp.zeros((half, half), F32)
    for i, reduced in enumerate(eliminate(schurs)):
        upper, inverse = split(reduced)
        if i == 0:
            upper_ref[half:, half:] = upper
        inverse_ref[i, half:, half:] = inverse
        inverse_ref[i, half:, :half] = -dot(inverse, sides[i])
    high_ref[0], low_ref[0] = halves(inverse_ref[0])
    last = inverse_ref[1]
    high_ref[1], low_ref[1] = halves(dot(last, last, (0, 0)))


def factor(pieces):
    count, _, order = pieces[0].shape
    return pl.pallas_call(
        factor_kernel,
        out_shape=[
            jax.ShapeDtypeStruct((order, order), F32),
            pltpu.HBM((count, order, order), BF16),
            pltpu.HBM((count, order, order), BF16),
        ],
        scratch_shapes=[pltpu.VMEM((count, order, order), F32)] * 2,
        cost_estimate=cost(16),
        compiler_params=room(8),
        name="factor",
    )(*pieces)


def cut(rows):
    sizes = [rows // 2] * 2
    return [pl.ds(sum(sizes[:i]), size) for i, size in enumerate(sizes)]


def project_kernel(sums_ref, *refs):
    (sh_from, sl_from, high_from, low_from, trailing_from, blocks_to, out_to), refs = refs[:7], refs[7:]
    sh_ref, sl_ref, high_ref, low_ref, trailing_ref, blocks_ref, out_ref, first, coming, going = refs
    stops, both, columns = sums_ref.shape
    height = both // 2
    rows = trailing_ref.shape[0]
    parts = cut(rows)
    chunks = len(parts)
    solves = [
        pltpu.make_async_copy(sh_from, sh_ref, first.at[0]),
        pltpu.make_async_copy(sl_from, sl_ref, first.at[1]),
    ]
    for copy in solves:
        copy.start()
    arrivals = []
    for i, part in enumerate(parts):
        arrivals.append(
            [
                pltpu.make_async_copy(source.at[part], target.at[part], coming.at[i, k])
                for k, (source, target) in enumerate(
                    ((high_from, high_ref), (low_from, low_ref), (trailing_from, trailing_ref))
                )
            ]
        )
        for copy in arrivals[-1]:
            copy.start()
    total = halves(sums_ref[:, height:, :].reshape(stops * height, columns))
    prefix = halves(sums_ref[:, :height, :].reshape(stops * height, columns))
    for copy in solves:
        copy.wait()
    coeffs = halves(dot3((sh_ref[1], sl_ref[1]), total))
    blocks_ref[...] = dot3((sh_ref[0], sl_ref[0]), prefix)
    leaving = [pltpu.make_async_copy(blocks_ref, blocks_to, going.at[chunks])]
    leaving[0].start()
    for i, part in enumerate(parts):
        for copy in arrivals[i]:
            copy.wait()
        out_ref[part, :] = trailing_ref[part, :] - dot3((high_ref[part, :], low_ref[part, :]), coeffs)
        leaving.append(pltpu.make_async_copy(out_ref.at[part], out_to.at[part], going.at[i]))
        leaving[-1].start()
    for copy in leaving:
        copy.wait()


def project(solves, sums, high, low, trailing):
    rows, columns = trailing.shape
    width = high.shape[1]
    chunks = len(cut(rows))
    anywhere = pl.BlockSpec(memory_space=pl.ANY)
    return pl.pallas_call(
        project_kernel,
        in_specs=[pl.BlockSpec(memory_space=pltpu.VMEM)] + [anywhere] * 5,
        out_specs=[anywhere] * 2,
        out_shape=[pltpu.HBM((width, columns), F32), pltpu.HBM((rows, columns), F32)],
        scratch_shapes=[pltpu.VMEM(s.shape, BF16) for s in (*solves, high, low)]
        + [
            pltpu.VMEM((rows, columns), F32),
            pltpu.VMEM((width, columns), F32),
            pltpu.VMEM((rows, columns), F32),
            pltpu.SemaphoreType.DMA((2,)),
            pltpu.SemaphoreType.DMA((chunks, 3)),
            pltpu.SemaphoreType.DMA((chunks + 1,)),
        ],
        cost_estimate=cost(6),
        compiler_params=room(24),
        name="project",
    )(sums, *[in_hbm(v) for v in (*solves, high, low, trailing)])


def stages(panel_transposed, trailing):
    stops = lax.axis_size("row")
    high, low, own_gram = gather(from_chips(panel_transposed))
    width = high.shape[0]
    columns = trailing.shape[1]
    piece = own_gram.shape

    def exchange(value):
        return lax.all_to_all(value, "row", 0, 0, tiled=True)

    behind = from_stops_x(own_gram)
    own_cross = cross(high, low, *halve(trailing))
    pieces = exchange(own_cross.reshape(stops, width // stops, columns))

    prefix, total = small(group_kernel, [piece] * 2, own_gram, *behind)
    other = from_pair_z(total)
    prefix, total = small(pair_kernel, [piece] * 2, prefix, total, other)
    behind = from_pairs_z(total)
    (grams,) = small(pairs_kernel, [(2,) + piece], prefix, total, *behind)
    grams = from_chips(grams)
    high, low = turn(high, low)

    both = scan(pieces)
    sums = exchange(both)
    grams, both = lax.optimization_barrier((grams, both))
    stop_factors, *solves = factor(grams)
    stop_blocks, projected = project(solves, sums, high, low, trailing)
    return (stop_factors, stop_blocks, projected)


def solution(mesh):
    return jax.shard_map(
        stages,
        mesh=mesh,
        in_specs=(P("col", "row"), P("row", "col")),
        out_specs=(P("row", None), P("row", "col"), P("row", "col")),
        check_vma=False,
    )
```

```python
import functools

import jax
import jax.numpy as jnp
from jax import lax
from jax.experimental import pallas as pl
from jax.experimental.pallas import tpu as pltpu
from jax.sharding import PartitionSpec as P


HIGHEST = lax.Precision.HIGHEST
F32 = jnp.float32
BF16 = jnp.bfloat16
X = 4


def dot(left, right, dims=(1, 0), precision=HIGHEST):
    return lax.dot_general(
        left,
        right,
        (((dims[0],), (dims[1],)), ((), ())),
        precision=precision,
        preferred_element_type=F32,
    )


def halves(value):
    high = value.astype(BF16)
    return high, (value - high.astype(F32)).astype(BF16)


def dot3(left, right, dims=(1, 0)):
    (lh, ll), (rh, rl) = left, right
    default = lax.Precision.DEFAULT
    return dot(lh, rh, dims, default) + (dot(ll, rh, dims, default) + dot(lh, rl, dims, default))


def dot4(left, right, dims=(1, 0)):
    return dot3(left, right, dims) + dot(left[1], right[1], dims, lax.Precision.DEFAULT)


def room(mebibytes):
    return pltpu.CompilerParams(vmem_limit_bytes=mebibytes * 2**20)


def cost(us):
    return pl.CostEstimate(flops=int(us * 5e8), bytes_accessed=int(us * 1e6), transcendentals=0)


def in_hbm(value):
    return pltpu.with_memory_space_constraint(value, pltpu.HBM)


def rotate(value, axis, pairs):
    return lax.ppermute(value, axis, pairs)


def from_same_cores(value):
    count = lax.axis_size("col")
    return [value] + [rotate(value, "col", [(i, (i + 2 * k) % count) for i in range(count)]) for k in (1, 3, 2)]


def from_other_core(values):
    count = lax.axis_size("col")
    return [rotate(v, "col", [(i, i ^ 1) for i in range(count)]) for v in values]


def from_chips(value):
    sames = from_same_cores(value)
    return sames + from_other_core(sames)


def chip_offsets():
    me = lax.axis_index("col")
    count = lax.axis_size("col")
    chip, core = me // 2, lax.rem(me, 2)
    chips = count // 2
    steps = (0, 1, 3, 2)
    return [2 * lax.rem(chip + chips - k, chips) + (core if same else 1 - core) for same in (True, False) for k in steps]


def from_stops_x(value):
    count = lax.axis_size("row")
    return [
        rotate(value, "row", [(i, i - i % X + (i + k) % X) for i in range(count)]) for k in (1, 3, 2)
    ]


def from_pair_z(value):
    count = lax.axis_size("row")
    return rotate(value, "row", [(i, i ^ X) for i in range(count)])


def from_pairs_z(value):
    count = lax.axis_size("row")
    return [rotate(value, "row", [(i, (i + 2 * X * k) % count) for i in range(count)]) for k in (1, 3, 2)]


def gather_kernel(*refs, count):
    pieces, before, (high_ref, low_ref, gram_ref) = refs[:count], refs[count:-3], refs[-3:]
    height = pieces[0].shape[0]
    for piece, owner in zip(pieces, chip_offsets()):
        rows = pl.ds(pl.multiple_of(owner * height, height), height)
        high, low = halves(piece[...])
        high_ref[rows, :] = high
        low_ref[rows, :] = low
    gram = dot4(halves(pieces[0][...]), (high_ref[...], low_ref[...]), (1, 1))
    for earlier in before:
        gram = gram + earlier[...]
    gram_ref[...] = gram


def gather(pieces, *before):
    height, rows = pieces[0].shape
    width = height * len(pieces)
    shapes = [(width, rows, BF16), (width, rows, BF16), (height, width, F32)]
    return pl.pallas_call(
        functools.partial(gather_kernel, count=len(pieces)),
        out_shape=[jax.ShapeDtypeStruct((a, b), t) for a, b, t in shapes],
        cost_estimate=cost(2),
        compiler_params=room(12),
        name="gather",
    )(*pieces, *before)


def turn_kernel(*refs):
    pairs, outs = refs[:-2], refs[-2:]
    at = 0
    for high_ref, low_ref in zip(pairs[::2], pairs[1::2]):
        part = pl.ds(at, high_ref.shape[1])
        for out, ref in zip(outs, (high_ref, low_ref)):
            out[part, :] = ref[...].T
        at += high_ref.shape[1]


def turn(*parts):
    width = parts[0].shape[0]
    rows = sum(part.shape[1] for part in parts[::2])
    return pl.pallas_call(
        turn_kernel,
        out_shape=[pltpu.VMEM((rows, width), BF16), pltpu.HBM((rows, width), BF16)],
        cost_estimate=cost(3),
        compiler_params=room(8),
        name="turn",
    )(*parts)


def halve_kernel(value_ref, high_ref, low_ref):
    high_ref[...], low_ref[...] = halves(value_ref[...])


def halve(value):
    rows, columns = value.shape
    block = 256
    spec = pl.BlockSpec((block, columns), lambda i: (i, 0))
    shape = jax.ShapeDtypeStruct(value.shape, BF16)
    return pl.pallas_call(
        halve_kernel,
        grid=(rows // block,),
        in_specs=[spec],
        out_specs=[spec] * 2,
        out_shape=[shape] * 2,
        cost_estimate=cost(2),
        compiler_params=room(8),
        name="halve",
    )(in_hbm(value))


def cross_kernel(high_ref, low_ref, right_high_ref, right_low_ref, *refs, start):
    before, out_ref = refs[:-1], refs[-1]
    part = pl.ds(start, high_ref.shape[1])
    product = dot3((high_ref[...], low_ref[...]), (right_high_ref[part, :], right_low_ref[part, :]))
    for earlier in before:
        product = product + earlier[...]
    out_ref[...] = product


def cross(start, high, low, right_high, right_low, *before):
    return pl.pallas_call(
        functools.partial(cross_kernel, start=start),
        out_shape=jax.ShapeDtypeStruct((high.shape[0], right_high.shape[1]), F32),
        cost_estimate=cost(2),
        compiler_params=room(16),
        name="cross",
    )(high, low, right_high, right_low, *before)


def group_kernel(own_ref, one_ref, three_ref, two_ref, prefix_ref, total_ref):
    place = lax.rem(lax.axis_index("row"), X)
    own, one, two, three = own_ref[...], one_ref[...], two_ref[...], three_ref[...]
    prefix_ref[...] = (
        own + jnp.where(place >= 1, one, 0.0) + jnp.where(place >= 2, two, 0.0) + jnp.where(place >= 3, three, 0.0)
    )
    total_ref[...] = (own + one) + (two + three)


def pair_kernel(before_ref, total_ref, other_ref, prefix_ref, pair_ref):
    odd = lax.rem(lax.div(lax.axis_index("row"), X), 2)
    other = other_ref[...]
    prefix_ref[...] = before_ref[...] + jnp.where(odd == 1, other, 0.0)
    pair_ref[...] = total_ref[...] + other


def pairs_kernel(before_ref, own_ref, one_ref, three_ref, two_ref, out_ref):
    place = lax.div(lax.axis_index("row"), 2 * X)
    own, one, two, three = own_ref[...], one_ref[...], two_ref[...], three_ref[...]
    out_ref[0] = (
        before_ref[...]
        + jnp.where(place >= 1, one, 0.0)
        + jnp.where(place >= 2, two, 0.0)
        + jnp.where(place >= 3, three, 0.0)
    )
    out_ref[1] = (own + one) + (two + three)


def small(kernel, shapes, *values):
    return pl.pallas_call(
        kernel,
        out_shape=[jax.ShapeDtypeStruct(shape, F32) for shape in shapes],
        cost_estimate=cost(1),
        compiler_params=room(2),
    )(*values)


def scan_kernel(pieces_ref, out_ref):
    stops, height, _ = pieces_ref.shape
    total = pieces_ref[0]
    out_ref[0, :height] = total
    for s in range(1, stops):
        total = total + pieces_ref[s]
        out_ref[s, :height] = total
    for s in range(stops):
        out_ref[s, height:] = total


def scan(pieces):
    stops, height, columns = pieces.shape
    return pl.pallas_call(
        scan_kernel,
        out_shape=pltpu.HBM((stops, 2 * height, columns), F32),
        cost_estimate=cost(1),
        compiler_params=room(4),
        name="scan",
    )(pieces)


def eliminate(matrices):
    order = matrices[0].shape[0]
    count = order // 8
    full = (8, order)
    lane = lax.broadcasted_iota(jnp.int32, full, 1)
    sublane = lax.broadcasted_iota(jnp.int32, full, 0)
    grids = [[m[8 * g : 8 * g + 8, :] for g in range(count)] for m in matrices]
    for p in range(count):
        start = 8 * p
        inside = (lane >= start) & (lane < start + 8)
        for grid in grids:
            block = grid[p]
            columns = [jnp.broadcast_to(block[:, start + c : start + c + 1], full) for c in range(8)]
            entry = [[None] * r + [jnp.broadcast_to(columns[r][c : c + 1, :], full) for c in range(r, 8)] for r in range(8)]
            rows = [jnp.broadcast_to(block[r : r + 1, :], full) for r in range(8)]
            rows = [jnp.where(inside, jnp.where(lane == start + r, 1.0, 0.0), rows[r]) for r in range(8)]
            inverse, multiple = [], [[None] * 8 for _ in range(8)]
            for k in range(8):
                inverse.append(jnp.square(lax.rsqrt(entry[k][k])))
                for r in range(k + 1, 8):
                    multiple[r][k] = entry[k][r] * inverse[k]
                for r in range(k + 1, 8):
                    for c in range(r, 8):
                        entry[r][c] = entry[r][c] - multiple[r][k] * entry[k][c]
                    rows[r] = rows[r] - multiple[r][k] * rows[k]
            result = rows[0]
            for r in range(1, 8):
                result = jnp.where(sublane == r, rows[r], result)
            for c in range(8):
                column = entry[0][c]
                for r in range(1, c + 1):
                    column = jnp.where(sublane == r, entry[r][c], column)
                result = jnp.where((lane == start + c) & (sublane <= c), column, result)
            if p < count - 1:
                solved = [rows[k] * inverse[k] for k in range(8)]
                for k in range(6, -1, -1):
                    for r in range(k + 1, 8):
                        solved[k] = solved[k] - multiple[r][k] * solved[r]
                for g in range(p + 1, count):
                    value = jnp.where(inside, 0.0, grid[g])
                    for k in range(8):
                        value = value - jnp.broadcast_to(grid[g][:, start + k : start + k + 1], full) * solved[k]
                    grid[g] = value
            grid[p] = result
    return [jnp.concatenate(grid, 0) for grid in grids]


def split(reduced):
    order = reduced.shape[0]
    row = lax.broadcasted_iota(jnp.int32, (order, order), 0)
    column = lax.broadcasted_iota(jnp.int32, (order, order), 1)
    pivots = jnp.sum(jnp.where(row == column, reduced, 0.0), axis=1, keepdims=True)
    scale = lax.rsqrt(pivots)
    upper = jnp.where(row <= column, reduced, 0.0) * scale
    lower = jnp.where(row > column, reduced, jnp.where(row == column, 1.0, 0.0)) * scale
    return upper, lower


def factor_kernel(*refs):
    pieces, (upper_ref, high_ref, low_ref, gram_ref, inverse_ref) = refs[:-5], refs[-5:]
    count, height, order = pieces[0].shape
    half = order // 2
    for piece, owner in zip(pieces, chip_offsets()):
        gram_ref[:, pl.ds(pl.multiple_of(owner * height, height), height), :] = piece[...]
    tops = eliminate([gram_ref[i, :half, :half] for i in range(count)])
    schurs, sides = [], []
    for i, reduced in enumerate(tops):
        upper, inverse = split(reduced)
        across = dot(inverse, gram_ref[i, :half, half:])
        side = dot(gram_ref[i, half:, :half], inverse, (1, 1))
        schurs.append(gram_ref[i, half:, half:] - dot(side, across))
        sides.append(dot(side, inverse))
        if i == 0:
            upper_ref[:half, :half] = upper
            upper_ref[:half, half:] = across
            upper_ref[half:, :half] = jnp.zeros((half, half), F32)
        inverse_ref[i, :half, :half] = inverse
        inverse_ref[i, :half, half:] = jnp.zeros((half, half), F32)
    for i, reduced in enumerate(eliminate(schurs)):
        upper, inverse = split(reduced)
        if i == 0:
            upper_ref[half:, half:] = upper
        inverse_ref[i, half:, half:] = inverse
        inverse_ref[i, half:, :half] = -dot(inverse, sides[i])
    high_ref[0], low_ref[0] = halves(inverse_ref[0])
    last = inverse_ref[1]
    high_ref[1], low_ref[1] = halves(dot(last, last, (0, 0)))


def factor(pieces):
    count, _, order = pieces[0].shape
    vmem = pl.BlockSpec(memory_space=pltpu.VMEM)
    return pl.pallas_call(
        factor_kernel,
        in_specs=[vmem] * len(pieces),
        out_specs=[vmem] * 3,
        out_shape=[
            jax.ShapeDtypeStruct((order, order), F32),
            pltpu.VMEM((count, order, order), BF16),
            pltpu.VMEM((count, order, order), BF16),
        ],
        scratch_shapes=[pltpu.VMEM((count, order, order), F32)] * 2,
        cost_estimate=cost(16),
        compiler_params=room(8),
        name="factor",
    )(*pieces)


def project_kernel(sums_ref, sh_ref, sl_ref, high_ref, low_from, trailing_from, *refs):
    blocks_to, out_to, low_ref, trailing_ref, blocks_ref, out_ref, coming, going = refs
    stops, both, columns = sums_ref.shape
    height = both // 2
    parts = coming.shape[0]
    size = trailing_ref.shape[0] // parts
    cut = [pl.ds(i * size, size) for i in range(parts)]
    arriving = [
        [
            pltpu.make_async_copy(low_from.at[part], low_ref.at[part], coming.at[i, 0]),
            pltpu.make_async_copy(trailing_from.at[part], trailing_ref.at[part], coming.at[i, 1]),
        ]
        for i, part in enumerate(cut)
    ]
    for pair in arriving:
        for copy in pair:
            copy.start()
    total = halves(sums_ref[:, height:, :].reshape(stops * height, columns))
    coeffs = halves(dot3((sh_ref[1], sl_ref[1]), total))
    prefix = halves(sums_ref[:, :height, :].reshape(stops * height, columns))
    blocks_ref[...] = dot3((sh_ref[0], sl_ref[0]), prefix)
    leaving = [pltpu.make_async_copy(blocks_ref, blocks_to, going.at[parts])]
    leaving[0].start()
    for i, part in enumerate(cut):
        for copy in arriving[i]:
            copy.wait()
        out_ref[part, :] = trailing_ref[part, :] - dot3((high_ref[part, :], low_ref[part, :]), coeffs)
        leaving.append(pltpu.make_async_copy(out_ref.at[part], out_to.at[part], going.at[i]))
        leaving[-1].start()
    for copy in leaving:
        copy.wait()


def project(solves, sums, high, low, trailing):
    rows, columns = trailing.shape
    width = high.shape[1]
    parts = 4
    anywhere = pl.BlockSpec(memory_space=pl.ANY)
    return pl.pallas_call(
        project_kernel,
        in_specs=[pl.BlockSpec(memory_space=pltpu.VMEM)] * 4 + [anywhere] * 2,
        out_specs=[anywhere] * 2,
        out_shape=[pltpu.HBM((width, columns), F32), pltpu.HBM((rows, columns), F32)],
        scratch_shapes=[
            pltpu.VMEM((rows, width), BF16),
            pltpu.VMEM((rows, columns), F32),
            pltpu.VMEM((width, columns), F32),
            pltpu.VMEM((rows, columns), F32),
            pltpu.SemaphoreType.DMA((parts, 2)),
            pltpu.SemaphoreType.DMA((parts + 1,)),
        ],
        cost_estimate=cost(4),
        compiler_params=room(20),
        name="project",
    )(sums, *solves, high, in_hbm(low), in_hbm(trailing))


def stages(panel_transposed, trailing):
    stops = lax.axis_size("row")
    first = panel_transposed.shape[1] // 2
    early = from_chips(panel_transposed[:, :first])
    late = from_chips(panel_transposed[:, first:])
    high_a, low_a, own_gram = gather(early)
    high, low, own_gram = gather(late, own_gram)
    width = high.shape[0]
    columns = trailing.shape[1]
    piece = own_gram.shape

    def exchange(value):
        return lax.all_to_all(value, "row", 0, 0, tiled=True)

    behind = from_stops_x(own_gram)
    right = halve(trailing)
    own_cross = cross(0, high_a, low_a, *right)
    own_cross = cross(first, high, low, *right, own_cross)
    pieces = exchange(own_cross.reshape(stops, width // stops, columns))

    prefix, total = small(group_kernel, [piece] * 2, own_gram, *behind)
    other = from_pair_z(total)
    prefix, total = small(pair_kernel, [piece] * 2, prefix, total, other)
    behind = from_pairs_z(total)
    (grams,) = small(pairs_kernel, [(2,) + piece], prefix, total, *behind)
    grams = from_chips(grams)
    high, low = turn(high_a, low_a, high, low)

    both = scan(pieces)
    sums = exchange(both)
    grams, both = lax.optimization_barrier((grams, both))
    stop_factors, *solves = factor(grams)
    stop_blocks, projected = project(solves, sums, high, low, trailing)
    return (stop_factors, stop_blocks, projected)


def solution(mesh):
    return jax.shard_map(
        stages,
        mesh=mesh,
        in_specs=(P("col", "row"), P("row", "col")),
        out_specs=(P("row", None), P("row", "col"), P("row", "col")),
        check_vma=False,
    )
```

```python
import jax
import jax.numpy as jnp
from jax import lax
from jax.experimental import pallas as pl
from jax.experimental.pallas import tpu as pltpu
from jax.sharding import PartitionSpec as P


HIGHEST = lax.Precision.HIGHEST
F32 = jnp.float32
BF16 = jnp.bfloat16
X = 4


def dot(left, right, dims=(1, 0), precision=HIGHEST):
    return lax.dot_general(
        left,
        right,
        (((dims[0],), (dims[1],)), ((), ())),
        precision=precision,
        preferred_element_type=F32,
    )


def halves(value):
    high = value.astype(BF16)
    return high, (value - high.astype(F32)).astype(BF16)


def dot3(left, right, dims=(1, 0)):
    (lh, ll), (rh, rl) = left, right
    default = lax.Precision.DEFAULT
    return dot(lh, rh, dims, default) + (dot(ll, rh, dims, default) + dot(lh, rl, dims, default))


def dot4(left, right, dims=(1, 0)):
    return dot3(left, right, dims) + dot(left[1], right[1], dims, lax.Precision.DEFAULT)


def room(mebibytes):
    return pltpu.CompilerParams(vmem_limit_bytes=mebibytes * 2**20)


def cost(us):
    return pl.CostEstimate(flops=int(us * 5e8), bytes_accessed=int(us * 1e6), transcendentals=0)


def in_hbm(value):
    return pltpu.with_memory_space_constraint(value, pltpu.HBM)


def rotate(value, axis, pairs):
    return lax.ppermute(value, axis, pairs)


def from_chips(value):
    count = lax.axis_size("col")
    sames = [value] + [
        rotate(value, "col", [(i, (i + 2 * k) % count) for i in range(count)]) for k in (1, 3, 2)
    ]
    others = [rotate(v, "col", [(i, i ^ 1) for i in range(count)]) for v in sames]
    return sames + others


def chip_offsets():
    me = lax.axis_index("col")
    count = lax.axis_size("col")
    chip, core = me // 2, lax.rem(me, 2)
    chips = count // 2
    steps = (0, 1, 3, 2)
    return [2 * lax.rem(chip + chips - k, chips) + (core if same else 1 - core) for same in (True, False) for k in steps]


def from_stops_x(value):
    count = lax.axis_size("row")
    return [
        rotate(value, "row", [(i, i - i % X + (i + k) % X) for i in range(count)]) for k in (1, 3, 2)
    ]


def from_pair_z(value):
    count = lax.axis_size("row")
    return rotate(value, "row", [(i, i ^ X) for i in range(count)])


def from_pairs_z(value):
    count = lax.axis_size("row")
    return [rotate(value, "row", [(i, (i + 2 * X * k) % count) for i in range(count)]) for k in (1, 3, 2)]


def gather_kernel(panel_ref, *refs):
    pieces, (high_ref, low_ref, gram_ref, own_ref, arrived) = refs[:-5], refs[-5:]
    height = own_ref.shape[0]
    fetch = pltpu.make_async_copy(panel_ref, own_ref, arrived)
    fetch.start()
    owners = chip_offsets()

    def place(value, owner):
        rows = pl.ds(pl.multiple_of(owner * height, height), height)
        high, low = halves(value)
        high_ref[rows, :] = high
        low_ref[rows, :] = low

    for piece, owner in zip(pieces, owners[1:]):
        place(piece[...], owner)
    fetch.wait()
    place(own_ref[...], owners[0])
    gram_ref[...] = dot4(halves(own_ref[...]), (high_ref[...], low_ref[...]), (1, 1))


def gather(pieces):
    height, rows = pieces[0].shape
    width = height * len(pieces)
    shapes = [(width, rows, BF16), (width, rows, BF16), (height, width, F32)]
    return pl.pallas_call(
        gather_kernel,
        in_specs=[pl.BlockSpec(memory_space=pl.ANY)] + [pl.BlockSpec(memory_space=pltpu.VMEM)] * (len(pieces) - 1),
        out_shape=[jax.ShapeDtypeStruct((a, b), t) for a, b, t in shapes],
        scratch_shapes=[pltpu.VMEM((height, rows), F32), pltpu.SemaphoreType.DMA],
        cost_estimate=cost(4),
        compiler_params=room(16),
        name="gather",
    )(in_hbm(pieces[0]), *pieces[1:])


def turn_kernel(high_ref, low_ref, high_out, low_out):
    high_out[...] = high_ref[...].T
    low_out[...] = low_ref[...].T


def turn(high, low):
    width, rows = high.shape
    return pl.pallas_call(
        turn_kernel,
        out_shape=[pltpu.VMEM((rows, width), BF16), pltpu.HBM((rows, width), BF16)],
        cost_estimate=cost(3),
        compiler_params=room(8),
        name="turn",
    )(high, low)


def halve_kernel(value_ref, high_ref, low_ref):
    high_ref[...], low_ref[...] = halves(value_ref[...])


def halve(value):
    rows, columns = value.shape
    block = 256
    spec = pl.BlockSpec((block, columns), lambda i: (i, 0))
    shape = jax.ShapeDtypeStruct(value.shape, BF16)
    return pl.pallas_call(
        halve_kernel,
        grid=(rows // block,),
        in_specs=[spec],
        out_specs=[spec] * 2,
        out_shape=[shape] * 2,
        cost_estimate=cost(2),
        compiler_params=room(8),
        name="halve",
    )(in_hbm(value))


def cross_kernel(high_ref, low_ref, right_high_ref, right_low_ref, out_ref):
    out_ref[...] = dot3((high_ref[...], low_ref[...]), (right_high_ref[...], right_low_ref[...]))


def cross(high, low, right_high, right_low):
    return pl.pallas_call(
        cross_kernel,
        out_shape=jax.ShapeDtypeStruct((high.shape[0], right_high.shape[1]), F32),
        cost_estimate=cost(4),
        compiler_params=room(16),
        name="cross",
    )(high, low, right_high, right_low)


def group_kernel(own_ref, one_ref, three_ref, two_ref, prefix_ref, total_ref):
    place = lax.rem(lax.axis_index("row"), X)
    own, one, two, three = own_ref[...], one_ref[...], two_ref[...], three_ref[...]
    prefix_ref[...] = (
        own + jnp.where(place >= 1, one, 0.0) + jnp.where(place >= 2, two, 0.0) + jnp.where(place >= 3, three, 0.0)
    )
    total_ref[...] = (own + one) + (two + three)


def pair_kernel(before_ref, total_ref, other_ref, prefix_ref, pair_ref):
    odd = lax.rem(lax.div(lax.axis_index("row"), X), 2)
    other = other_ref[...]
    prefix_ref[...] = before_ref[...] + jnp.where(odd == 1, other, 0.0)
    pair_ref[...] = total_ref[...] + other


def pairs_kernel(before_ref, own_ref, one_ref, three_ref, two_ref, out_ref):
    place = lax.div(lax.axis_index("row"), 2 * X)
    own, one, two, three = own_ref[...], one_ref[...], two_ref[...], three_ref[...]
    out_ref[0] = (
        before_ref[...]
        + jnp.where(place >= 1, one, 0.0)
        + jnp.where(place >= 2, two, 0.0)
        + jnp.where(place >= 3, three, 0.0)
    )
    out_ref[1] = (own + one) + (two + three)


def small(kernel, shapes, *values):
    return pl.pallas_call(
        kernel,
        out_shape=[jax.ShapeDtypeStruct(shape, F32) for shape in shapes],
        cost_estimate=cost(1),
        compiler_params=room(2),
    )(*values)


def scan_kernel(pieces_ref, out_ref):
    stops, height, _ = pieces_ref.shape
    total = pieces_ref[0]
    out_ref[0, :height] = total
    for s in range(1, stops):
        total = total + pieces_ref[s]
        out_ref[s, :height] = total
    for s in range(stops):
        out_ref[s, height:] = total


def scan(pieces):
    stops, height, columns = pieces.shape
    return pl.pallas_call(
        scan_kernel,
        out_shape=pltpu.HBM((stops, 2 * height, columns), F32),
        cost_estimate=cost(1),
        compiler_params=room(4),
        name="scan",
    )(pieces)


def eliminate(matrices):
    order = matrices[0].shape[0]
    count = order // 8
    full = (8, order)
    lane = lax.broadcasted_iota(jnp.int32, full, 1)
    sublane = lax.broadcasted_iota(jnp.int32, full, 0)
    grids = [[m[8 * g : 8 * g + 8, :] for g in range(count)] for m in matrices]
    for p in range(count):
        start = 8 * p
        inside = (lane >= start) & (lane < start + 8)
        for grid in grids:
            block = grid[p]
            columns = [jnp.broadcast_to(block[:, start + c : start + c + 1], full) for c in range(8)]
            entry = [[None] * r + [jnp.broadcast_to(columns[r][c : c + 1, :], full) for c in range(r, 8)] for r in range(8)]
            rows = [jnp.broadcast_to(block[r : r + 1, :], full) for r in range(8)]
            rows = [jnp.where(inside, jnp.where(lane == start + r, 1.0, 0.0), rows[r]) for r in range(8)]
            inverse, multiple = [], [[None] * 8 for _ in range(8)]
            for k in range(8):
                inverse.append(jnp.square(lax.rsqrt(entry[k][k])))
                for r in range(k + 1, 8):
                    multiple[r][k] = entry[k][r] * inverse[k]
                for r in range(k + 1, 8):
                    for c in range(r, 8):
                        entry[r][c] = entry[r][c] - multiple[r][k] * entry[k][c]
                    rows[r] = rows[r] - multiple[r][k] * rows[k]
            result = rows[0]
            for r in range(1, 8):
                result = jnp.where(sublane == r, rows[r], result)
            for c in range(8):
                column = entry[0][c]
                for r in range(1, c + 1):
                    column = jnp.where(sublane == r, entry[r][c], column)
                result = jnp.where((lane == start + c) & (sublane <= c), column, result)
            if p < count - 1:
                solved = [rows[k] * inverse[k] for k in range(8)]
                for k in range(6, -1, -1):
                    for r in range(k + 1, 8):
                        solved[k] = solved[k] - multiple[r][k] * solved[r]
                for g in range(p + 1, count):
                    value = jnp.where(inside, 0.0, grid[g])
                    for k in range(8):
                        value = value - jnp.broadcast_to(grid[g][:, start + k : start + k + 1], full) * solved[k]
                    grid[g] = value
            grid[p] = result
    return [jnp.concatenate(grid, 0) for grid in grids]


def split(reduced):
    order = reduced.shape[0]
    row = lax.broadcasted_iota(jnp.int32, (order, order), 0)
    column = lax.broadcasted_iota(jnp.int32, (order, order), 1)
    pivots = jnp.sum(jnp.where(row == column, reduced, 0.0), axis=1, keepdims=True)
    scale = lax.rsqrt(pivots)
    upper = jnp.where(row <= column, reduced, 0.0) * scale
    lower = jnp.where(row > column, reduced, jnp.where(row == column, 1.0, 0.0)) * scale
    return upper, lower


def factor_kernel(*refs):
    pieces, (upper_ref, high_ref, low_ref, gram_ref, inverse_ref) = refs[:-5], refs[-5:]
    count, height, order = pieces[0].shape
    half = order // 2
    for piece, owner in zip(pieces, chip_offsets()):
        gram_ref[:, pl.ds(pl.multiple_of(owner * height, height), height), :] = piece[...]
    tops = eliminate([gram_ref[i, :half, :half] for i in range(count)])
    schurs, sides = [], []
    for i, reduced in enumerate(tops):
        upper, inverse = split(reduced)
        across = dot(inverse, gram_ref[i, :half, half:])
        side = dot(gram_ref[i, half:, :half], inverse, (1, 1))
        schurs.append(gram_ref[i, half:, half:] - dot(side, across))
        sides.append(dot(side, inverse))
        if i == 0:
            upper_ref[:half, :half] = upper
            upper_ref[:half, half:] = across
            upper_ref[half:, :half] = jnp.zeros((half, half), F32)
        inverse_ref[i, :half, :half] = inverse
        inverse_ref[i, :half, half:] = jnp.zeros((half, half), F32)
    for i, reduced in enumerate(eliminate(schurs)):
        upper, inverse = split(reduced)
        if i == 0:
            upper_ref[half:, half:] = upper
        inverse_ref[i, half:, half:] = inverse
        inverse_ref[i, half:, :half] = -dot(inverse, sides[i])
    high_ref[0], low_ref[0] = halves(inverse_ref[0])
    last = inverse_ref[1]
    high_ref[1], low_ref[1] = halves(dot(last, last, (0, 0)))


def factor(pieces):
    count, _, order = pieces[0].shape
    vmem = pl.BlockSpec(memory_space=pltpu.VMEM)
    return pl.pallas_call(
        factor_kernel,
        in_specs=[vmem] * len(pieces),
        out_specs=[vmem] * 3,
        out_shape=[
            jax.ShapeDtypeStruct((order, order), F32),
            pltpu.VMEM((count, order, order), BF16),
            pltpu.VMEM((count, order, order), BF16),
        ],
        scratch_shapes=[pltpu.VMEM((count, order, order), F32)] * 2,
        cost_estimate=cost(16),
        compiler_params=room(8),
        name="factor",
    )(*pieces)


def project_kernel(sums_ref, sh_ref, sl_ref, high_ref, low_from, trailing_from, *refs):
    blocks_to, out_to, low_ref, trailing_ref, blocks_ref, out_ref, coming, going = refs
    stops, both, columns = sums_ref.shape
    height = both // 2
    parts = coming.shape[0]
    size = trailing_ref.shape[0] // parts
    cut = [pl.ds(i * size, size) for i in range(parts)]
    arriving = [
        [
            pltpu.make_async_copy(low_from.at[part], low_ref.at[part], coming.at[i, 0]),
            pltpu.make_async_copy(trailing_from.at[part], trailing_ref.at[part], coming.at[i, 1]),
        ]
        for i, part in enumerate(cut)
    ]
    for pair in arriving:
        for copy in pair:
            copy.start()
    total = halves(sums_ref[:, height:, :].reshape(stops * height, columns))
    coeffs = halves(dot3((sh_ref[1], sl_ref[1]), total))
    prefix = halves(sums_ref[:, :height, :].reshape(stops * height, columns))
    blocks_ref[...] = dot3((sh_ref[0], sl_ref[0]), prefix)
    leaving = [pltpu.make_async_copy(blocks_ref, blocks_to, going.at[parts])]
    leaving[0].start()
    for i, part in enumerate(cut):
        for copy in arriving[i]:
            copy.wait()
        out_ref[part, :] = trailing_ref[part, :] - dot3((high_ref[part, :], low_ref[part, :]), coeffs)
        leaving.append(pltpu.make_async_copy(out_ref.at[part], out_to.at[part], going.at[i]))
        leaving[-1].start()
    for copy in leaving:
        copy.wait()


def project(solves, sums, high, low, trailing):
    rows, columns = trailing.shape
    width = high.shape[1]
    parts = 4
    anywhere = pl.BlockSpec(memory_space=pl.ANY)
    return pl.pallas_call(
        project_kernel,
        in_specs=[pl.BlockSpec(memory_space=pltpu.VMEM)] * 4 + [anywhere] * 2,
        out_specs=[anywhere] * 2,
        out_shape=[pltpu.HBM((width, columns), F32), pltpu.HBM((rows, columns), F32)],
        scratch_shapes=[
            pltpu.VMEM((rows, width), BF16),
            pltpu.VMEM((rows, columns), F32),
            pltpu.VMEM((width, columns), F32),
            pltpu.VMEM((rows, columns), F32),
            pltpu.SemaphoreType.DMA((parts, 2)),
            pltpu.SemaphoreType.DMA((parts + 1,)),
        ],
        cost_estimate=cost(4),
        compiler_params=room(20),
        name="project",
    )(sums, *solves, high, in_hbm(low), in_hbm(trailing))


def stages(panel_transposed, trailing):
    stops = lax.axis_size("row")
    high, low, own_gram = gather(from_chips(panel_transposed))
    width = high.shape[0]
    columns = trailing.shape[1]
    piece = own_gram.shape

    def exchange(value):
        return lax.all_to_all(value, "row", 0, 0, tiled=True)

    behind = from_stops_x(own_gram)
    own_cross = cross(high, low, *halve(trailing))
    pieces = exchange(own_cross.reshape(stops, width // stops, columns))

    prefix, total = small(group_kernel, [piece] * 2, own_gram, *behind)
    other = from_pair_z(total)
    prefix, total = small(pair_kernel, [piece] * 2, prefix, total, other)
    behind = from_pairs_z(total)
    (grams,) = small(pairs_kernel, [(2,) + piece], prefix, total, *behind)
    grams = from_chips(grams)
    high, low = turn(high, low)

    both = scan(pieces)
    sums = exchange(both)
    grams, both = lax.optimization_barrier((grams, both))
    stop_factors, *solves = factor(grams)
    stop_blocks, projected = project(solves, sums, high, low, trailing)
    return (stop_factors, stop_blocks, projected)


def solution(mesh):
    return jax.shard_map(
        stages,
        mesh=mesh,
        in_specs=(P("col", "row"), P("row", "col")),
        out_specs=(P("row", None), P("row", "col"), P("row", "col")),
        check_vma=False,
    )
```
